128 devices in a mesh: rep: 4 (over z), shard: 16 (over x, y_lo, core), tp: 2 (over y_hi).
Axes of the slice: x: 4, y: 4 (y_hi: 2, y_lo: 2; y = y_hi * 2 + y_lo), z: 4, core: 2. Of those that a mesh axis runs over, the one named last changes fastest.
Arguments:
- delta_inputs: bfloat16 [4, 2, 768, 2304], P('rep', None, 'shard', 'tp'), may hold values from -6 to 6
- delta_mixing: bfloat16 [4, 2, 768, 768], P('rep', None, 'shard', 'tp'), may hold values from -6 to 6
- delta_expand: bfloat16 [4, 2, 768, 3072], P('rep', None, 'shard', 'tp'), may hold values from -6 to 6
- delta_reduce: bfloat16 [4, 2, 3072, 768], P('rep', None, 'shard', 'tp'), may hold values from -6 to 6
- owner_weights: float32 [4, 16, 2, 110592], P('rep', 'shard', 'tp'), may hold values from -6 to 6
- owner_momentum: float32 [4, 16, 2, 110592], P('rep', 'shard', 'tp'), may hold values from -6 to 6
- delta_embed: bfloat16 [4, 50304, 768], P('rep', 'shard', 'tp'), may hold values from -6 to 6
- embed_owner: float32 [16, 4, 786, 768], P('shard', 'rep', None, 'tp'), may hold values from -6 to 6
- embed_momentum: float32 [16, 4, 786, 64], P('shard', 'rep'), may hold values from -6 to 6
- basis: float32 [768, 64], P('tp'), may hold values from -0.21875 to 0.21875
Outputs:
- fresh_inputs: bfloat16 [2, 768, 2304], P(None, 'shard', 'tp')
- fresh_mixing: bfloat16 [2, 768, 768], P(None, 'shard', 'tp')
- fresh_expand: bfloat16 [2, 768, 3072], P(None, 'shard', 'tp')
- fresh_reduce: bfloat16 [2, 3072, 768], P(None, 'shard', 'tp')
- next_weights: float32 [4, 16, 2, 110592], P('rep', 'shard', 'tp')
- next_momentum: float32 [4, 16, 2, 110592], P('rep', 'shard', 'tp')
- fresh_embed: bfloat16 [50304, 768], P('shard', 'tp')
- next_embed: float32 [16, 4, 786, 768], P('shard', 'rep', None, 'tp')
- next_embed_momentum: float32 [16, 4, 786, 64], P('shard', 'rep')
The draws below stay inside these ranges and needn't reach their ends.
All inputs are finite; a program needn't handle non-finite values.
Results may differ from the reference program's by a relative error of at most 0.0085.
Values may be sent and summed in bfloat16 or wider, within the bound.
A program may use at most 64 MiB of HBM per device.

```python
import jax
import jax.numpy as jnp
from jax import lax

D = 768
FF = 3072
VOCAB = 50304
RANK = 64
LAYERS = 2
FLAT = 110592
N_REP = 4
N_SHARD = 16
N_TP = 2


def block_levels(rng, shape, cuts, low, top_value):
    level, own = 1.0, jax.random.fold_in(rng, 6)
    for dim, shards_of in cuts:
        steps = jnp.exp(jax.random.uniform(jax.random.fold_in(own, dim), (shards_of,), jnp.float32, low / len(cuts), top_value / len(cuts)))
        level = level * jnp.repeat(steps, shape[dim] // shards_of).reshape([-1 if axis == dim else 1 for axis in range(len(shape))])
    return level


def normal_values(stream_key, dims, spread, most, shards=(), kind=jnp.bfloat16):
    drawn = spread * jax.random.normal(stream_key, dims, jnp.float32)
    if shards:
        drawn = drawn * block_levels(stream_key, dims, shards, -0.22, 0.18)
    return jnp.clip(drawn, -most, most).astype(kind)


def setup_inputs(seed: int = 0) -> dict:
    splits = jax.random.split(jax.random.key(seed), 11)
    delta_inputs = normal_values(splits[0], (N_REP, LAYERS, D, 3 * D), 1.0, 6.0, ((0, 4), (2, 16), (3, 2)))
    delta_mixing = normal_values(splits[1], (N_REP, LAYERS, D, D), 1.0, 6.0, ((0, 4), (2, 16), (3, 2)))
    delta_expand = normal_values(splits[2], (N_REP, LAYERS, D, FF), 1.0, 6.0, ((0, 4), (2, 16), (3, 2)))
    delta_reduce = normal_values(splits[3], (N_REP, LAYERS, FF, D), 1.0, 6.0, ((0, 4), (2, 16), (3, 2)))
    owner_weights = normal_values(splits[4], (N_REP, N_SHARD, N_TP, FLAT), 1.0, 6.0, ((0, 4), (1, 16), (2, 2)), jnp.float32)
    owner_momentum = normal_values(splits[5], (N_REP, N_SHARD, N_TP, FLAT), 1.0, 6.0, ((0, 4), (1, 16), (2, 2)), jnp.float32)
    delta_embed = normal_values(splits[6], (N_REP, VOCAB, D), 1.0, 6.0, ((0, 4), (1, 16), (2, 2)))
    embed_owner = normal_values(splits[7], (N_SHARD, N_REP, VOCAB // (N_SHARD * N_REP), D), 1.0, 6.0, ((0, 16), (1, 4), (3, 2)), jnp.float32)
    embed_momentum = normal_values(splits[8], (N_SHARD, N_REP, VOCAB // (N_SHARD * N_REP), RANK), 1.0, 6.0, ((0, 16), (1, 4)), jnp.float32)
    basis = normal_values(splits[9], (D, RANK), D ** -0.5, 0.21875, ((0, 2),), jnp.float32)
    return {"delta_inputs": delta_inputs, "delta_mixing": delta_mixing, "delta_expand": delta_expand, "delta_reduce": delta_reduce, "owner_weights": owner_weights, "owner_momentum": owner_momentum, "delta_embed": delta_embed, "embed_owner": embed_owner, "embed_momentum": embed_momentum, "basis": basis}


MOMENTUM = 0.5
OUTER_RATE = 0.7


def to_owner(array, rows, cols):
    sub = rows // (N_SHARD * N_REP)
    piece = cols // (N_TP * N_SHARD)
    view = array.reshape(LAYERS, N_SHARD, N_REP, sub, N_TP, N_SHARD, piece)
    view = jnp.transpose(view, (2, 5, 4, 0, 3, 1, 6))
    return view.reshape(N_REP, N_SHARD, N_TP, LAYERS * sub * N_SHARD * piece)


def from_owner(flat_part, rows, cols):
    sub = rows // (N_SHARD * N_REP)
    piece = cols // (N_TP * N_SHARD)
    view = flat_part.reshape(N_REP, N_SHARD, N_TP, LAYERS, sub, N_SHARD, piece)
    view = jnp.transpose(view, (3, 5, 0, 4, 2, 1, 6))
    return view.reshape(LAYERS, rows, cols)


def reference(delta_inputs, delta_mixing, delta_expand, delta_reduce, owner_weights, owner_momentum, delta_embed, embed_owner, embed_momentum, basis):
    deltas = (delta_inputs, delta_mixing, delta_expand, delta_reduce)
    shapes = ((D, 3 * D), (D, D), (D, FF), (FF, D))
    pieces = []
    for delta, shape in zip(deltas, shapes):
        mean_value = jnp.sum(delta, axis=0, dtype=jnp.float32) / N_REP
        pieces.append(to_owner(mean_value, shape[0], shape[1]))
    gradient = jnp.concatenate(pieces, axis=3)
    next_momentum = MOMENTUM * owner_momentum + gradient
    next_weights = owner_weights - OUTER_RATE * (gradient + MOMENTUM * next_momentum)
    copies = next_weights.astype(jnp.bfloat16)
    fresh = []
    offset = 0
    for shape in shapes:
        count = LAYERS * shape[0] * shape[1] // (N_REP * N_SHARD * N_TP)
        fresh.append(from_owner(copies[..., offset:offset + count], shape[0], shape[1]))
        offset = offset + count
    embed_mean = jnp.sum(delta_embed, axis=0, dtype=jnp.float32) / N_REP
    coefficients = jnp.dot(embed_mean, basis, precision=lax.Precision.HIGHEST, preferred_element_type=jnp.float32)
    momentum_rows = MOMENTUM * embed_momentum.reshape(VOCAB, RANK) + coefficients
    direction = coefficients + MOMENTUM * momentum_rows
    table = embed_owner.reshape(VOCAB, D) - OUTER_RATE * jnp.dot(direction, basis.T, precision=lax.Precision.HIGHEST, preferred_element_type=jnp.float32)
    fresh_embed = table.astype(jnp.bfloat16)
    next_embed = table.reshape(embed_owner.shape)
    next_embed_momentum = momentum_rows.reshape(embed_momentum.shape)
    return (fresh[0], fresh[1], fresh[2], fresh[3], next_weights, next_momentum, fresh_embed, next_embed, next_embed_momentum)
```

```python
import jax
import jax.numpy as jnp
from jax import lax
from jax.experimental import pallas as pl
from jax.experimental.pallas import tpu as pltpu
from jax.sharding import PartitionSpec as P

MOMENTUM = 0.5
OUTER_RATE = 0.7
MESH = pl.DeviceIdType.MESH
F32 = jnp.float32
BF16 = jnp.bfloat16

GROUPS = 4
PEERS = 16
ROWS = 786
VROWS = 3144
WIDTH = 384
RANK = 64
FLAT_ROWS = 864
PACK = 416
HALF = 208
STAGE = 800
CHUNK = 448

W_IN, W_MIX, W_EXP, W_RED = 72, 24, 96, 24


def lanes(rows):
    return lax.broadcasted_iota(jnp.int32, (rows, 128), 1)


def tile(x, index):
    return x[:, index * 128 : (index + 1) * 128]


def turn(x, shift):
    shift = shift % 128
    return x if shift == 0 else pltpu.roll(x, shift, 1)


def place(total, lane, x, low, high):
    if total is None:
        return x
    return jnp.where((lane >= low) & (lane < high), x, total)


def piece(total, lane, src, start, width, to):
    first, last = start // 128, (start + width - 1) // 128
    shift = to - start % 128
    cut = width if first == last else last * 128 - start
    total = place(total, lane, turn(tile(src, first), shift), to, to + cut)
    if first != last:
        total = place(total, lane, turn(tile(src, last), shift), to + cut, to + width)
    return total


def split_columns(kinds, send_ref):
    inputs, mixing, expand, reduces = kinds
    lane = lanes(24)
    for u in range(PEERS):
        a = piece(None, lane, inputs, u * W_IN, W_IN, 0)
        a = piece(a, lane, mixing, u * W_MIX, W_MIX, W_IN)
        b = piece(None, lane, expand, u * W_EXP, W_EXP, 0)
        c = None
        for j in range(4):
            c = piece(c, lane, reduces[j], u * W_RED, W_RED, j * W_RED)
        send_ref[u] = jnp.concatenate([a, b, c], axis=1).astype(BF16)


def merge_columns(recv_ref):
    lane = lanes(24)
    blocks = [recv_ref[s].astype(F32) for s in range(PEERS)]

    def kind(which, width, base):
        out = []
        for t in range(PEERS * width // 128):
            total = None
            for s in range(PEERS):
                low, high = max(s * width - t * 128, 0), min((s + 1) * width - t * 128, 128)
                if low >= high:
                    continue
                shifted = turn(tile(blocks[s], which), s * width - t * 128 - base)
                total = place(total, lane, shifted, low, high)
            out.append(total)
        return out

    return (
        kind(0, W_IN, 0),
        kind(0, W_MIX, W_IN),
        kind(1, W_EXP, 0),
        [kind(2, W_RED, j * W_RED) for j in range(4)],
    )


def to_flat(kinds, flat_ref):
    inputs, mixing, expand, reduces = kinds
    for base, tiles in (
        [(0, inputs), (216, mixing), (288, expand)] + [(576 + 72 * j, reduces[j]) for j in range(4)]
    ):
        count = len(tiles)
        for t in range(count):
            flat_ref[pl.ds(base + t, 24, count), :] = tiles[t]


def from_flat(flat_ref):
    def rows(base, count):
        return jnp.concatenate(
            [flat_ref[pl.ds(base + t, 24, count), :] for t in range(count)], axis=1
        )

    return rows(0, 9), rows(216, 3), rows(288, 12), [rows(576 + 72 * j, 3) for j in range(4)]


def kinds_of(top, low):
    inputs, mixing = top[:24], top[24:, :384]
    expand = jnp.concatenate([low[:24], low[24:, :384]], axis=1)
    reduces = [top[24:, 384:768], top[24:, 768:], low[24:, 384:768], low[24:, 768:]]
    return inputs, mixing, expand, reduces


def halves_of(inputs, mixing, expand, reduces):
    top = jnp.concatenate(
        [inputs, jnp.concatenate([mixing, reduces[0], reduces[1]], axis=1)], axis=0
    )
    low = jnp.concatenate(
        [
            expand[:, :1152],
            jnp.concatenate([expand[:, 1152:], reduces[2], reduces[3]], axis=1),
        ],
        axis=0,
    )
    return top, low


def kernel(
    din_h, dmix_h, dexp_h, dred_h, w_h, m_h, de_h, eo_h, em_h, basis_h,
    fin_h, fmix_h, fexp_h, fred_h, wn_h, mn_h, fe_h, ne_h, nem_h,
    din, dmix, dexp, dred, w, m, de, eo, em, basis,
    fin, fmix, fexp, fred, wn, mn, fe, ne, nem,
    rs_send, rs_mid, rs_merge, rs_recv,
    a1_send, a1_recv, a2_send, a2_recv, flat, ag,
    coef, cf_send, cf_mid, cf_merge, cf_recv, tp_send, tp_recv, stage,
    in_sem, out_sem, z_send, z_recv, a1_ss, a1_rs, a2_ss, a2_rs, tp_ss, tp_rs,
):
    r, s, t = lax.axis_index("rep"), lax.axis_index("shard"), lax.axis_index("tp")
    right, left, opp = (r + 1) % GROUPS, (r + 3) % GROUPS, (r + 2) % GROUPS

    ins = [
        pltpu.make_async_copy(a, b, in_sem.at[i])
        for i, (a, b) in enumerate(
            [(din_h, din), (dmix_h, dmix), (dexp_h, dexp), (dred_h, dred), (basis_h, basis),
             (de_h, de), (em_h, em), (eo_h, eo), (w_h, w), (m_h, m)]
        )
    ]
    for c in ins:
        c.start()

    barrier = pltpu.get_barrier_semaphore()
    for z in (right, left):
        pl.semaphore_signal(barrier, inc=1, device_id={"rep": z}, device_id_type=MESH)
    for d in range(1, PEERS):
        pl.semaphore_signal(
            barrier, inc=1, device_id={"shard": (s + d) % PEERS}, device_id_type=MESH
        )
    pl.semaphore_signal(barrier, inc=1, device_id={"tp": 1 - t}, device_id_type=MESH)

    count = [0]

    def z_copy(src, dst, to):
        i = count[0]
        count[0] += 1
        return pltpu.make_async_remote_copy(
            src_ref=src, dst_ref=dst, send_sem=z_send.at[i], recv_sem=z_recv.at[i],
            device_id={"rep": to}, device_id_type=MESH,
        )

    for c in ins[:4]:
        c.wait()

    def pack(q, ref):
        return jnp.concatenate(
            [ref[l].astype(F32)[12 * q : 12 * q + 12] for l in range(2)], axis=0
        )

    for q in range(GROUPS):
        red = [dred[l, pl.ds(48 * q, 48), :].astype(F32) for l in range(2)]
        top, low = halves_of(
            pack(q, din), pack(q, dmix), pack(q, dexp),
            [red[0][:24], red[0][24:], red[1][:24], red[1][24:]],
        )
        rs_send[q, 0] = top.astype(BF16)
        rs_send[q, 1] = low.astype(BF16)

    pl.semaphore_wait(barrier, PEERS + 2)
    rs1 = [z_copy(rs_send.at[opp, 0], rs_mid.at[0], right),
           z_copy(rs_send.at[opp, 1], rs_mid.at[1], left)]
    for c in rs1:
        c.start()

    ins[4].wait()
    b = basis[...]
    b_hi = b.astype(BF16)
    b_lo = (b - b_hi.astype(F32)).astype(BF16)
    rhs = jnp.concatenate([b_hi, b_hi, b_lo, b_lo], axis=1)
    ins[5].wait()

    def terms(start, rows):
        y = jnp.dot(de[pl.ds(start, rows), :], rhs, preferred_element_type=F32)
        coef[pl.ds(start, rows), :] = y[:, :128] + y[:, 128:]

    def body(i, carry):
        terms(pl.multiple_of(i * CHUNK, CHUNK), CHUNK)
        return carry

    lax.fori_loop(0, VROWS // CHUNK, body, 0)
    terms(VROWS // CHUNK * CHUNK, VROWS % CHUNK)
    coef[pl.ds(VROWS, 56), :] = jnp.zeros((56, 128), F32)
    lane = lanes(PACK)
    for q in range(GROUPS):
        packed = jnp.where(
            lane < RANK, coef[pl.ds(ROWS * q, PACK), :], coef[pl.ds(ROWS * q + PACK, PACK), :]
        ).astype(BF16)
        cf_send[q, 0] = packed[:HALF]
        cf_send[q, 1] = packed[HALF:]
    cf1 = [z_copy(cf_send.at[opp, 0], cf_mid.at[0], right),
           z_copy(cf_send.at[opp, 1], cf_mid.at[1], left)]
    cf2 = [z_copy(cf_send.at[right, 1], cf_recv.at[1], right),
           z_copy(cf_send.at[left, 0], cf_recv.at[3], left)]
    rs2 = [z_copy(rs_send.at[right, 1], rs_recv.at[1], right),
           z_copy(rs_send.at[left, 0], rs_recv.at[3], left)]
    for c in cf1 + cf2 + rs2:
        c.start()

    for c in cf1:
        c.wait_recv()
    cf_merge[0] = (cf_send[right, 0].astype(F32) + cf_mid[0].astype(F32)).astype(BF16)
    cf_merge[1] = (cf_send[left, 1].astype(F32) + cf_mid[1].astype(F32)).astype(BF16)
    cf3 = [z_copy(cf_merge.at[0], cf_recv.at[0], right),
           z_copy(cf_merge.at[1], cf_recv.at[2], left)]
    for c in cf3:
        c.start()

    for c in rs1:
        c.wait_recv()
    rs_merge[0] = (rs_send[right, 0].astype(F32) + rs_mid[0].astype(F32)).astype(BF16)
    rs_merge[1] = (rs_send[left, 1].astype(F32) + rs_mid[1].astype(F32)).astype(BF16)
    rs3 = [z_copy(rs_merge.at[0], rs_recv.at[0], right),
           z_copy(rs_merge.at[1], rs_recv.at[2], left)]
    for c in rs3:
        c.start()

    for c in cf2 + cf3:
        c.wait_recv()

    def total(send, recv):
        top = send[r, 0].astype(F32) + (recv[0].astype(F32) + recv[3].astype(F32))
        low = send[r, 1].astype(F32) + (recv[1].astype(F32) + recv[2].astype(F32))
        return top, low

    top, low = total(cf_send, cf_recv)
    tp_send[pl.ds(0, HALF), :] = top.astype(BF16)
    tp_send[pl.ds(HALF, HALF), :] = low.astype(BF16)
    tp = pltpu.make_async_remote_copy(
        src_ref=tp_send, dst_ref=tp_recv, send_sem=tp_ss.at[0], recv_sem=tp_rs.at[0],
        device_id={"tp": 1 - t}, device_id_type=MESH,
    )
    tp.start()

    def exchange(send, recv, send_sem, recv_sem):
        copies = [
            pltpu.make_async_remote_copy(
                src_ref=send.at[(s + d) % PEERS], dst_ref=recv.at[s],
                send_sem=send_sem.at[d], recv_sem=recv_sem.at[d],
                device_id={"shard": (s + d) % PEERS}, device_id_type=MESH,
            )
            for d in range(1, PEERS)
        ]
        for c in copies:
            c.start()
        recv[s] = send[s]
        return copies

    for c in rs2 + rs3:
        c.wait_recv()
    top, low = total(rs_send, rs_recv)
    split_columns(kinds_of(top * 0.25, low * 0.25), a1_send)
    a1 = exchange(a1_send, a1_recv, a1_ss, a1_rs)

    for c in ins[6:8]:
        c.wait()
    tp.wait_recv()
    both = (tp_send[...].astype(F32) + tp_recv[...].astype(F32)) * 0.25
    dims = (((1,), (1,)), ((), ()))
    for start, rows, c in ((0, PACK, both), (PACK, ROWS - PACK, turn(both, RANK))):
        c = c[:rows, :RANK]
        momentum = MOMENTUM * em[pl.ds(start, rows), :] + c
        nem[pl.ds(start, rows), :] = momentum
        direction = c + MOMENTUM * momentum
        d_hi = direction.astype(BF16)
        d_lo = (direction - d_hi.astype(F32)).astype(BF16)
        update = lax.dot_general(d_hi, b_hi, dims, preferred_element_type=F32)
        update += lax.dot_general(d_lo, b_hi, dims, preferred_element_type=F32)
        update += lax.dot_general(d_hi, b_lo, dims, preferred_element_type=F32)
        table = eo[pl.ds(start, rows), :] - OUTER_RATE * update
        ne[pl.ds(start, rows), :] = table
        stage[r, pl.ds(start, rows), :] = table.astype(BF16)
    first, second = pl.ds(0, STAGE // 2), pl.ds(STAGE // 2, STAGE // 2)
    eg1 = [z_copy(stage.at[r, first], stage.at[r, first], right),
           z_copy(stage.at[r, second], stage.at[r, second], left)]
    eg2 = [z_copy(stage.at[r, second], stage.at[r, second], right),
           z_copy(stage.at[r, first], stage.at[r, first], left)]
    for c in eg1 + eg2:
        c.start()
    outs = [pltpu.make_async_copy(a, o, out_sem.at[i])
            for i, (a, o) in enumerate([(nem, nem_h), (ne, ne_h), (mn, mn_h), (wn, wn_h),
                                        (fin, fin_h), (fmix, fmix_h), (fexp, fexp_h),
                                        (fred, fred_h), (fe, fe_h)])]
    for c in outs[:2]:
        c.start()

    for c in ins[8:10]:
        c.wait()
    for c in a1:
        c.wait_recv()
    to_flat(merge_columns(a1_recv), flat)
    gradient = flat[...]
    momentum = MOMENTUM * m[...] + gradient
    mn[...] = momentum
    wn[...] = w[...] - OUTER_RATE * (gradient + MOMENTUM * momentum)
    split_columns(from_flat(wn), a2_send)
    a2 = exchange(a2_send, a2_recv, a2_ss, a2_rs)
    for c in outs[2:4]:
        c.start()

    for c in a2:
        c.wait_recv()
    inputs, mixing, expand, reduces = merge_columns(a2_recv)
    join = lambda tiles: jnp.concatenate(tiles, axis=1)
    top, low = halves_of(join(inputs), join(mixing), join(expand), [join(x) for x in reduces])
    ag[r, 0] = top.astype(BF16)
    ag[r, 1] = low.astype(BF16)
    dg1 = [z_copy(ag.at[r, 0], ag.at[r, 0], right), z_copy(ag.at[r, 1], ag.at[r, 1], left)]
    dg2 = [z_copy(ag.at[r, 1], ag.at[r, 1], right), z_copy(ag.at[r, 0], ag.at[r, 0], left)]
    for c in dg1 + dg2:
        c.start()

    for c in eg1:
        c.wait_recv()
    eg3 = [z_copy(stage.at[left, first], stage.at[left, first], right),
           z_copy(stage.at[right, second], stage.at[right, second], left)]
    for c in eg3:
        c.start()
    for c in dg1:
        c.wait_recv()
    dg3 = [z_copy(ag.at[left, 0], ag.at[left, 0], right),
           z_copy(ag.at[right, 1], ag.at[right, 1], left)]
    for c in dg3:
        c.start()

    for c in eg2 + eg3:
        c.wait_recv()
    for q in range(GROUPS):
        fe[pl.ds(ROWS * q, ROWS), :] = stage[q, pl.ds(0, ROWS), :]
    outs[8].start()

    for c in dg2 + dg3:
        c.wait_recv()
    parts = [kinds_of(ag[q, 0].astype(F32), ag[q, 1].astype(F32)) for q in range(GROUPS)]
    for l in range(2):
        for k, out in enumerate((fin, fmix, fexp)):
            out[l] = jnp.concatenate(
                [parts[q][k][12 * l : 12 * l + 12] for q in range(GROUPS)], axis=0
            ).astype(BF16)
        for q in range(GROUPS):
            fred[l, pl.ds(48 * q, 48), :] = jnp.concatenate(
                [parts[q][3][2 * l], parts[q][3][2 * l + 1]], axis=0
            ).astype(BF16)
    for c in outs[4:8]:
        c.start()

    for c in (rs1 + rs2 + rs3 + cf1 + cf2 + cf3 + [tp] + a1 + a2 + eg1 + eg2 + eg3
              + dg1 + dg2 + dg3):
        c.wait_send()
    for c in outs:
        c.wait()


def local(
    delta_inputs, delta_mixing, delta_expand, delta_reduce, owner_weights, owner_momentum,
    delta_embed, embed_owner, embed_momentum, basis,
):
    args = (
        delta_inputs[0], delta_mixing[0], delta_expand[0], delta_reduce[0],
        owner_weights.reshape(FLAT_ROWS, 128), owner_momentum.reshape(FLAT_ROWS, 128),
        delta_embed[0], embed_owner[0, 0], embed_momentum[0, 0], basis,
    )
    outs = (
        args[0], args[1], args[2], args[3], args[4], args[5], args[6], args[7], args[8],
    )
    vmem = lambda x: pltpu.VMEM(x.shape, x.dtype)
    dma = pltpu.SemaphoreType.DMA
    half = (48, 1152)
    results = pl.pallas_call(
        kernel,
        name="outer_step",
        out_shape=[jax.ShapeDtypeStruct(x.shape, x.dtype) for x in outs],
        in_specs=[pl.BlockSpec(memory_space=pl.ANY)] * 10,
        out_specs=[pl.BlockSpec(memory_space=pl.ANY)] * 9,
        scratch_shapes=[vmem(x) for x in args]
        + [vmem(x) for x in outs]
        + [
            pltpu.VMEM((GROUPS, 2) + half, BF16),
            pltpu.VMEM((2,) + half, BF16),
            pltpu.VMEM((2,) + half, BF16),
            pltpu.VMEM((4,) + half, BF16),
            pltpu.VMEM((PEERS, 24, 384), BF16),
            pltpu.VMEM((PEERS, 24, 384), BF16),
            pltpu.VMEM((PEERS, 24, 384), BF16),
            pltpu.VMEM((PEERS, 24, 384), BF16),
            pltpu.VMEM((FLAT_ROWS, 128), F32),
            pltpu.VMEM((GROUPS, 2) + half, BF16),
            pltpu.VMEM((VROWS + 56, 128), F32),
            pltpu.VMEM((GROUPS, 2, HALF, 128), BF16),
            pltpu.VMEM((2, HALF, 128), BF16),
            pltpu.VMEM((2, HALF, 128), BF16),
            pltpu.VMEM((4, HALF, 128), BF16),
            pltpu.VMEM((PACK, 128), BF16),
            pltpu.VMEM((PACK, 128), BF16),
            pltpu.VMEM((GROUPS, STAGE, WIDTH), BF16),
            dma((10,)),
            dma((9,)),
            dma((24,)),
            dma((24,)),
            dma((PEERS,)),
            dma((PEERS,)),
            dma((PEERS,)),
            dma((PEERS,)),
            dma((1,)),
            dma((1,)),
        ],
        compiler_params=pltpu.CompilerParams(
            collective_id=0, has_side_effects=True, vmem_limit_bytes=48 * 1024 * 1024
        ),
    )(*args)
    return (
        results[0], results[1], results[2], results[3],
        results[4].reshape(owner_weights.shape), results[5].reshape(owner_momentum.shape),
        results[6], results[7][None, None], results[8][None, None],
    )


def solution(mesh):
    in_specs = (
        P("rep", None, "shard", "tp"),
        P("rep", None, "shard", "tp"),
        P("rep", None, "shard", "tp"),
        P("rep", None, "shard", "tp"),
        P("rep", "shard", "tp", None),
        P("rep", "shard", "tp", None),
        P("rep", "shard", "tp"),
        P("shard", "rep", None, "tp"),
        P("shard", "rep", None, None),
        P("tp", None),
    )
    out_specs = (
        P(None, "shard", "tp"),
        P(None, "shard", "tp"),
        P(None, "shard", "tp"),
        P(None, "shard", "tp"),
        P("rep", "shard", "tp", None),
        P("rep", "shard", "tp", None),
        P("shard", "tp"),
        P("shard", "rep", None, "tp"),
        P("shard", "rep", None, None),
    )
    return jax.shard_map(local, mesh=mesh, in_specs=in_specs, out_specs=out_specs, check_vma=False)
```

```python
import jax
import jax.numpy as jnp
from jax import lax
from jax.experimental import pallas as pl
from jax.experimental.pallas import tpu as pltpu
from jax.sharding import PartitionSpec as P

MOMENTUM = 0.5
OUTER_RATE = 0.7
MESH = pl.DeviceIdType.MESH
F32 = jnp.float32
BF16 = jnp.bfloat16

GROUPS = 4
PEERS = 16
ROWS = 786
VROWS = 3144
WIDTH = 384
RANK = 64
FLAT_ROWS = 864
PACK = 416
HALF = 208
STAGE = 800
CHUNK = 448

W_IN, W_MIX, W_EXP, W_RED = 72, 24, 96, 24


def lanes(rows):
    return lax.broadcasted_iota(jnp.int32, (rows, 128), 1)


def tile(x, index):
    return x[:, index * 128 : (index + 1) * 128]


def turn(x, shift):
    shift = shift % 128
    return x if shift == 0 else pltpu.roll(x, shift, 1)


def place(total, lane, x, low, high):
    if total is None:
        return x
    return jnp.where((lane >= low) & (lane < high), x, total)


def piece(total, lane, src, start, width, to):
    first, last = start // 128, (start + width - 1) // 128
    shift = to - start % 128
    cut = width if first == last else last * 128 - start
    total = place(total, lane, turn(tile(src, first), shift), to, to + cut)
    if first != last:
        total = place(total, lane, turn(tile(src, last), shift), to + cut, to + width)
    return total


def split_columns(kinds, send_ref):
    inputs, mixing, expand, reduces = kinds
    lane = lanes(24)
    for u in range(PEERS):
        a = piece(None, lane, inputs, u * W_IN, W_IN, 0)
        a = piece(a, lane, mixing, u * W_MIX, W_MIX, W_IN)
        b = piece(None, lane, expand, u * W_EXP, W_EXP, 0)
        c = None
        for j in range(4):
            c = piece(c, lane, reduces[j], u * W_RED, W_RED, j * W_RED)
        send_ref[u] = jnp.concatenate([a, b, c], axis=1).astype(BF16)


def merge_columns(recv_ref):
    lane = lanes(24)
    blocks = [recv_ref[s].astype(F32) for s in range(PEERS)]

    def kind(which, width, base):
        out = []
        for t in range(PEERS * width // 128):
            total = None
            for s in range(PEERS):
                low, high = max(s * width - t * 128, 0), min((s + 1) * width - t * 128, 128)
                if low >= high:
                    continue
                shifted = turn(tile(blocks[s], which), s * width - t * 128 - base)
                total = place(total, lane, shifted, low, high)
            out.append(total)
        return out

    return (
        kind(0, W_IN, 0),
        kind(0, W_MIX, W_IN),
        kind(1, W_EXP, 0),
        [kind(2, W_RED, j * W_RED) for j in range(4)],
    )


def to_flat(kinds, flat_ref):
    inputs, mixing, expand, reduces = kinds
    for base, tiles in (
        [(0, inputs), (216, mixing), (288, expand)] + [(576 + 72 * j, reduces[j]) for j in range(4)]
    ):
        count = len(tiles)
        for t in range(count):
            flat_ref[pl.ds(base + t, 24, count), :] = tiles[t]


def from_flat(flat_ref):
    def rows(base, count):
        return jnp.concatenate(
            [flat_ref[pl.ds(base + t, 24, count), :] for t in range(count)], axis=1
        )

    return rows(0, 9), rows(216, 3), rows(288, 12), [rows(576 + 72 * j, 3) for j in range(4)]


def kinds_of(top, low):
    inputs, mixing = top[:24], top[24:, :384]
    expand = jnp.concatenate([low[:24], low[24:, :384]], axis=1)
    reduces = [top[24:, 384:768], top[24:, 768:], low[24:, 384:768], low[24:, 768:]]
    return inputs, mixing, expand, reduces


def halves_of(inputs, mixing, expand, reduces):
    top = jnp.concatenate(
        [inputs, jnp.concatenate([mixing, reduces[0], reduces[1]], axis=1)], axis=0
    )
    low = jnp.concatenate(
        [
            expand[:, :1152],
            jnp.concatenate([expand[:, 1152:], reduces[2], reduces[3]], axis=1),
        ],
        axis=0,
    )
    return top, low


def kernel(
    din_h, dmix_h, dexp_h, dred_h, w_h, m_h, de_h, eo_h, em_h, basis_h,
    fin_h, fmix_h, fexp_h, fred_h, wn_h, mn_h, fe_h, ne_h, nem_h,
    din, dmix, dexp, dred, w, m, de, eo, em, basis,
    fin, fmix, fexp, fred, wn, mn, fe, ne, nem,
    rs_send, rs_mid, rs_merge, rs_recv,
    a1_send, a1_recv, a2_send, a2_recv, flat, ag,
    coef, cf_send, cf_mid, cf_merge, cf_recv, tp_send, tp_recv, stage,
    in_sem, out_sem, z_send, z_recv, a1_ss, a1_rs, a2_ss, a2_rs, tp_ss, tp_rs,
):
    r, s, t = lax.axis_index("rep"), lax.axis_index("shard"), lax.axis_index("tp")
    right, left, opp = (r + 1) % GROUPS, (r + 3) % GROUPS, (r + 2) % GROUPS

    ins = [
        pltpu.make_async_copy(a, b, in_sem.at[i])
        for i, (a, b) in enumerate(
            [(din_h, din), (dmix_h, dmix), (dexp_h, dexp), (dred_h, dred), (basis_h, basis),
             (de_h, de), (em_h, em), (eo_h.at[:, 0, :], eo), (w_h, w), (m_h, m)]
        )
    ]
    for c in ins:
        c.start()

    barrier = pltpu.get_barrier_semaphore()
    for z in (right, left):
        pl.semaphore_signal(barrier, inc=1, device_id={"rep": z}, device_id_type=MESH)
    for d in range(1, PEERS):
        pl.semaphore_signal(
            barrier, inc=1, device_id={"shard": (s + d) % PEERS}, device_id_type=MESH
        )
    pl.semaphore_signal(barrier, inc=1, device_id={"tp": 1 - t}, device_id_type=MESH)

    count = [0]

    def z_copy(src, dst, to):
        i = count[0]
        count[0] += 1
        return pltpu.make_async_remote_copy(
            src_ref=src, dst_ref=dst, send_sem=z_send.at[i], recv_sem=z_recv.at[i],
            device_id={"rep": to}, device_id_type=MESH,
        )

    for c in ins[:4]:
        c.wait()

    def pack(q, ref):
        return jnp.concatenate(
            [ref[l].astype(F32)[12 * q : 12 * q + 12] for l in range(2)], axis=0
        )

    for q in range(GROUPS):
        red = [dred[l, pl.ds(48 * q, 48), :].astype(F32) for l in range(2)]
        top, low = halves_of(
            pack(q, din), pack(q, dmix), pack(q, dexp),
            [red[0][:24], red[0][24:], red[1][:24], red[1][24:]],
        )
        rs_send[q, 0] = top.astype(BF16)
        rs_send[q, 1] = low.astype(BF16)

    pl.semaphore_wait(barrier, PEERS + 2)
    rs1 = [z_copy(rs_send.at[opp, 0], rs_mid.at[0], right),
           z_copy(rs_send.at[opp, 1], rs_mid.at[1], left)]
    for c in rs1:
        c.start()

    ins[4].wait()
    b = basis[...]
    b_hi = b.astype(BF16)
    b_lo = (b - b_hi.astype(F32)).astype(BF16)
    rhs = jnp.concatenate([b_hi, b_hi, b_lo, b_lo], axis=0)
    across = (((1,), (1,)), ((), ()))
    ins[5].wait()

    def terms(start, rows):
        y = lax.dot_general(
            de[pl.ds(start, rows), :], rhs, across, preferred_element_type=F32
        )
        coef[pl.ds(start, rows), :] = y[:, :128] + y[:, 128:]

    def body(i, carry):
        terms(pl.multiple_of(i * CHUNK, CHUNK), CHUNK)
        return carry

    lax.fori_loop(0, VROWS // CHUNK, body, 0)
    terms(VROWS // CHUNK * CHUNK, VROWS % CHUNK)
    coef[pl.ds(VROWS, 56), :] = jnp.zeros((56, 128), F32)
    lane = lanes(PACK)
    for q in range(GROUPS):
        packed = jnp.where(
            lane < RANK, coef[pl.ds(ROWS * q, PACK), :], coef[pl.ds(ROWS * q + PACK, PACK), :]
        ).astype(BF16)
        cf_send[q, 0] = packed[:HALF]
        cf_send[q, 1] = packed[HALF:]
    cf1 = [z_copy(cf_send.at[opp, 0], cf_mid.at[0], right),
           z_copy(cf_send.at[opp, 1], cf_mid.at[1], left)]
    cf2 = [z_copy(cf_send.at[right, 1], cf_recv.at[1], right),
           z_copy(cf_send.at[left, 0], cf_recv.at[3], left)]
    rs2 = [z_copy(rs_send.at[right, 1], rs_recv.at[1], right),
           z_copy(rs_send.at[left, 0], rs_recv.at[3], left)]
    for c in cf1 + cf2 + rs2:
        c.start()

    for c in cf1:
        c.wait_recv()
    cf_merge[0] = (cf_send[right, 0].astype(F32) + cf_mid[0].astype(F32)).astype(BF16)
    cf_merge[1] = (cf_send[left, 1].astype(F32) + cf_mid[1].astype(F32)).astype(BF16)
    cf3 = [z_copy(cf_merge.at[0], cf_recv.at[0], right),
           z_copy(cf_merge.at[1], cf_recv.at[2], left)]
    for c in cf3:
        c.start()

    for c in rs1:
        c.wait_recv()
    rs_merge[0] = (rs_send[right, 0].astype(F32) + rs_mid[0].astype(F32)).astype(BF16)
    rs_merge[1] = (rs_send[left, 1].astype(F32) + rs_mid[1].astype(F32)).astype(BF16)
    rs3 = [z_copy(rs_merge.at[0], rs_recv.at[0], right),
           z_copy(rs_merge.at[1], rs_recv.at[2], left)]
    for c in rs3:
        c.start()

    for c in cf2 + cf3:
        c.wait_recv()

    def total(send, recv):
        top = send[r, 0].astype(F32) + (recv[0].astype(F32) + recv[3].astype(F32))
        low = send[r, 1].astype(F32) + (recv[1].astype(F32) + recv[2].astype(F32))
        return top, low

    top, low = total(cf_send, cf_recv)
    tp_send[pl.ds(0, HALF), :] = top.astype(BF16)
    tp_send[pl.ds(HALF, HALF), :] = low.astype(BF16)
    tp = pltpu.make_async_remote_copy(
        src_ref=tp_send, dst_ref=tp_recv, send_sem=tp_ss.at[0], recv_sem=tp_rs.at[0],
        device_id={"tp": 1 - t}, device_id_type=MESH,
    )
    tp.start()

    def exchange(send, recv, send_sem, recv_sem):
        copies = [
            pltpu.make_async_remote_copy(
                src_ref=send.at[(s + d) % PEERS], dst_ref=recv.at[s],
                send_sem=send_sem.at[d], recv_sem=recv_sem.at[d],
                device_id={"shard": (s + d) % PEERS}, device_id_type=MESH,
            )
            for d in range(1, PEERS)
        ]
        for c in copies:
            c.start()
        recv[s] = send[s]
        return copies

    for c in rs2 + rs3:
        c.wait_recv()
    top, low = total(rs_send, rs_recv)
    split_columns(kinds_of(top * 0.25, low * 0.25), a1_send)
    a1 = exchange(a1_send, a1_recv, a1_ss, a1_rs)

    for c in ins[6:8]:
        c.wait()
    tp.wait_recv()
    both = (tp_send[...].astype(F32) + tp_recv[...].astype(F32)) * 0.25
    momenta = jnp.transpose(em[...])
    kept = []
    for start, rows, c in ((0, PACK, both), (PACK, ROWS - PACK, turn(both, RANK))):
        c = c[:rows, :RANK]
        momentum = MOMENTUM * momenta[start : start + rows] + c
        kept.append(momentum)
        direction = c + MOMENTUM * momentum
        d_hi = direction.astype(BF16)
        d_lo = (direction - d_hi.astype(F32)).astype(BF16)
        update = jnp.dot(d_hi, b_hi, preferred_element_type=F32)
        update += jnp.dot(d_lo, b_hi, preferred_element_type=F32)
        update += jnp.dot(d_hi, b_lo, preferred_element_type=F32)
        parts = []
        for j in range(WIDTH // 128):
            place_of = pl.ds(3 * start + j, rows, 3)
            table = eo[place_of, :] - OUTER_RATE * tile(update, j)
            ne[place_of, :] = table
            parts.append(table.astype(BF16))
        stage[r, pl.ds(start, rows), :] = jnp.concatenate(parts, axis=1)
    first, second = pl.ds(0, STAGE // 2), pl.ds(STAGE // 2, STAGE // 2)
    eg1 = [z_copy(stage.at[r, first], stage.at[r, first], right),
           z_copy(stage.at[r, second], stage.at[r, second], left)]
    eg2 = [z_copy(stage.at[r, second], stage.at[r, second], right),
           z_copy(stage.at[r, first], stage.at[r, first], left)]
    for c in eg1 + eg2:
        c.start()
    nem[...] = jnp.transpose(jnp.concatenate(kept, axis=0))
    outs = [pltpu.make_async_copy(a, o, out_sem.at[i])
            for i, (a, o) in enumerate([(nem, nem_h), (ne, ne_h), (mn, mn_h), (wn, wn_h),
                                        (fin, fin_h), (fmix, fmix_h), (fexp, fexp_h),
                                        (fred, fred_h), (fe, fe_h)])]
    for c in outs[:2]:
        c.start()

    for c in ins[8:10]:
        c.wait()
    for c in a1:
        c.wait_recv()
    to_flat(merge_columns(a1_recv), flat)
    gradient = flat[...]
    momentum = MOMENTUM * m[...] + gradient
    mn[...] = momentum
    wn[...] = w[...] - OUTER_RATE * (gradient + MOMENTUM * momentum)
    split_columns(from_flat(wn), a2_send)
    a2 = exchange(a2_send, a2_recv, a2_ss, a2_rs)
    for c in outs[2:4]:
        c.start()

    for c in a2:
        c.wait_recv()
    inputs, mixing, expand, reduces = merge_columns(a2_recv)
    join = lambda tiles: jnp.concatenate(tiles, axis=1)
    top, low = halves_of(join(inputs), join(mixing), join(expand), [join(x) for x in reduces])
    ag[r, 0] = top.astype(BF16)
    ag[r, 1] = low.astype(BF16)
    dg1 = [z_copy(ag.at[r, 0], ag.at[r, 0], right), z_copy(ag.at[r, 1], ag.at[r, 1], left)]
    dg2 = [z_copy(ag.at[r, 1], ag.at[r, 1], right), z_copy(ag.at[r, 0], ag.at[r, 0], left)]
    for c in dg1 + dg2:
        c.start()

    for c in eg1:
        c.wait_recv()
    eg3 = [z_copy(stage.at[left, first], stage.at[left, first], right),
           z_copy(stage.at[right, second], stage.at[right, second], left)]
    for c in eg3:
        c.start()
    for c in dg1:
        c.wait_recv()
    dg3 = [z_copy(ag.at[left, 0], ag.at[left, 0], right),
           z_copy(ag.at[right, 1], ag.at[right, 1], left)]
    for c in dg3:
        c.start()

    for c in eg2 + eg3:
        c.wait_recv()
    for q in range(GROUPS):
        fe[pl.ds(ROWS * q, ROWS), :] = stage[q, pl.ds(0, ROWS), :]
    outs[8].start()

    for c in dg2 + dg3:
        c.wait_recv()
    parts = [kinds_of(ag[q, 0].astype(F32), ag[q, 1].astype(F32)) for q in range(GROUPS)]
    for l in range(2):
        for k, out in enumerate((fin, fmix, fexp)):
            out[l] = jnp.concatenate(
                [parts[q][k][12 * l : 12 * l + 12] for q in range(GROUPS)], axis=0
            ).astype(BF16)
        for q in range(GROUPS):
            fred[l, pl.ds(48 * q, 48), :] = jnp.concatenate(
                [parts[q][3][2 * l], parts[q][3][2 * l + 1]], axis=0
            ).astype(BF16)
    for c in outs[4:8]:
        c.start()

    for c in (rs1 + rs2 + rs3 + cf1 + cf2 + cf3 + [tp] + a1 + a2 + eg1 + eg2 + eg3
              + dg1 + dg2 + dg3):
        c.wait_send()
    for c in outs:
        c.wait()


def flush(*refs):
    sem = refs[18]
    copies = []
    for i in range(9):
        to = refs[9 + i].at[:, 0, :] if i == 7 else refs[9 + i]
        copies.append(pltpu.make_async_copy(refs[i], to, sem.at[i]))
    for c in copies:
        c.start()
    for c in copies:
        c.wait()


def local(
    delta_inputs, delta_mixing, delta_expand, delta_reduce, owner_weights, owner_momentum,
    delta_embed, embed_owner, embed_momentum, basis,
):
    args = (
        delta_inputs[0], delta_mixing[0], delta_expand[0], delta_reduce[0],
        owner_weights.reshape(FLAT_ROWS, 128), owner_momentum.reshape(FLAT_ROWS, 128),
        delta_embed[0],
        jnp.transpose(embed_owner[0], (1, 0, 2)).reshape(3 * ROWS, 1, 128),
        embed_momentum[0, 0].T, basis.T,
    )
    table = jax.ShapeDtypeStruct((3 * ROWS, 128), F32)
    outs = args[:7] + (table, args[8])
    vmem = lambda x: pltpu.VMEM(x.shape, x.dtype)
    dma = pltpu.SemaphoreType.DMA
    half = (48, 1152)
    args = tuple(pltpu.with_memory_space_constraint(x, pltpu.HBM) for x in args)
    results = pl.pallas_call(
        kernel,
        name="outer_step",
        out_shape=[jax.ShapeDtypeStruct(x.shape, x.dtype) for x in outs],
        in_specs=[pl.BlockSpec(memory_space=pltpu.HBM)] * 10,
        out_specs=[pl.BlockSpec(memory_space=pl.ANY)] * 9,
        scratch_shapes=[vmem(x) for x in args[:7] + (table,) + args[8:]]
        + [vmem(x) for x in outs]
        + [
            pltpu.VMEM((GROUPS, 2) + half, BF16),
            pltpu.VMEM((2,) + half, BF16),
            pltpu.VMEM((2,) + half, BF16),
            pltpu.VMEM((4,) + half, BF16),
            pltpu.VMEM((PEERS, 24, 384), BF16),
            pltpu.VMEM((PEERS, 24, 384), BF16),
            pltpu.VMEM((PEERS, 24, 384), BF16),
            pltpu.VMEM((PEERS, 24, 384), BF16),
            pltpu.VMEM((FLAT_ROWS, 128), F32),
            pltpu.VMEM((GROUPS, 2) + half, BF16),
            pltpu.VMEM((VROWS + 56, 128), F32),
            pltpu.VMEM((GROUPS, 2, HALF, 128), BF16),
            pltpu.VMEM((2, HALF, 128), BF16),
            pltpu.VMEM((2, HALF, 128), BF16),
            pltpu.VMEM((4, HALF, 128), BF16),
            pltpu.VMEM((PACK, 128), BF16),
            pltpu.VMEM((PACK, 128), BF16),
            pltpu.VMEM((GROUPS, STAGE, WIDTH), BF16),
            dma((10,)),
            dma((9,)),
            dma((24,)),
            dma((24,)),
            dma((PEERS,)),
            dma((PEERS,)),
            dma((PEERS,)),
            dma((PEERS,)),
            dma((1,)),
            dma((1,)),
        ],
        compiler_params=pltpu.CompilerParams(
            collective_id=0, has_side_effects=True, vmem_limit_bytes=26 * 1024 * 1024
        ),
    )(*args)
    results = pl.pallas_call(
        flush,
        name="flush",
        out_shape=[jax.ShapeDtypeStruct(x.shape, x.dtype) for x in args[:9]],
        in_specs=[pl.BlockSpec(memory_space=pl.ANY)] * 9,
        out_specs=[pl.BlockSpec(memory_space=pl.ANY)] * 9,
        scratch_shapes=[dma((9,))],
        compiler_params=pltpu.CompilerParams(vmem_limit_bytes=1024 * 1024),
    )(*results)
    return (
        results[0], results[1], results[2], results[3],
        results[4].reshape(owner_weights.shape), results[5].reshape(owner_momentum.shape),
        results[6],
        jnp.transpose(results[7].reshape(ROWS, 1, WIDTH), (1, 0, 2))[None],
        results[8].T[None, None],
    )


def solution(mesh):
    in_specs = (
        P("rep", None, "shard", "tp"),
        P("rep", None, "shard", "tp"),
        P("rep", None, "shard", "tp"),
        P("rep", None, "shard", "tp"),
        P("rep", "shard", "tp", None),
        P("rep", "shard", "tp", None),
        P("rep", "shard", "tp"),
        P("shard", "rep", None, "tp"),
        P("shard", "rep", None, None),
        P("tp", None),
    )
    out_specs = (
        P(None, "shard", "tp"),
        P(None, "shard", "tp"),
        P(None, "shard", "tp"),
        P(None, "shard", "tp"),
        P("rep", "shard", "tp", None),
        P("rep", "shard", "tp", None),
        P("shard", "tp"),
        P("shard", "rep", None, "tp"),
        P("shard", "rep", None, None),
    )
    return jax.shard_map(local, mesh=mesh, in_specs=in_specs, out_specs=out_specs, check_vma=False)
```

```python
import jax
import jax.numpy as jnp
from jax import lax
from jax.experimental import pallas as pl
from jax.experimental.pallas import tpu as pltpu
from jax.sharding import PartitionSpec as P

MOMENTUM = 0.5
OUTER_RATE = 0.7
MESH = pl.DeviceIdType.MESH
F32 = jnp.float32
BF16 = jnp.bfloat16

GROUPS = 4
PEERS = 16
ROWS = 786
VROWS = 3144
WIDTH = 384
RANK = 64
FLAT_ROWS = 864
PACK = 416
HALF = 208
STAGE = 800
CHUNK = 448

W_IN, W_MIX, W_EXP, W_RED = 72, 24, 96, 24


def lanes(rows):
    return lax.broadcasted_iota(jnp.int32, (rows, 128), 1)


def tile(x, index):
    return x[:, index * 128 : (index + 1) * 128]


def turn(x, shift):
    shift = shift % 128
    return x if shift == 0 else pltpu.roll(x, shift, 1)


def place(total, lane, x, low, high):
    if total is None:
        return x
    return jnp.where((lane >= low) & (lane < high), x, total)


def piece(total, lane, src, start, width, to):
    first, last = start // 128, (start + width - 1) // 128
    shift = to - start % 128
    cut = width if first == last else last * 128 - start
    total = place(total, lane, turn(tile(src, first), shift), to, to + cut)
    if first != last:
        total = place(total, lane, turn(tile(src, last), shift), to + cut, to + width)
    return total


def split_columns(kinds, send_ref):
    inputs, mixing, expand, reduces = kinds
    lane = lanes(24)
    for u in range(PEERS):
        a = piece(None, lane, inputs, u * W_IN, W_IN, 0)
        a = piece(a, lane, mixing, u * W_MIX, W_MIX, W_IN)
        b = piece(None, lane, expand, u * W_EXP, W_EXP, 0)
        c = None
        for j in range(4):
            c = piece(c, lane, reduces[j], u * W_RED, W_RED, j * W_RED)
        send_ref[u] = jnp.concatenate([a, b, c], axis=1).astype(BF16)


def merge_columns(recv_ref):
    lane = lanes(24)
    blocks = [recv_ref[s].astype(F32) for s in range(PEERS)]

    def kind(which, width, base):
        out = []
        for t in range(PEERS * width // 128):
            total = None
            for s in range(PEERS):
                low, high = max(s * width - t * 128, 0), min((s + 1) * width - t * 128, 128)
                if low >= high:
                    continue
                shifted = turn(tile(blocks[s], which), s * width - t * 128 - base)
                total = place(total, lane, shifted, low, high)
            out.append(total)
        return out

    return (
        kind(0, W_IN, 0),
        kind(0, W_MIX, W_IN),
        kind(1, W_EXP, 0),
        [kind(2, W_RED, j * W_RED) for j in range(4)],
    )


def to_flat(kinds, flat_ref):
    inputs, mixing, expand, reduces = kinds
    for base, tiles in (
        [(0, inputs), (216, mixing), (288, expand)] + [(576 + 72 * j, reduces[j]) for j in range(4)]
    ):
        count = len(tiles)
        for t in range(count):
            flat_ref[pl.ds(base + t, 24, count), :] = tiles[t]


def from_flat(flat_ref):
    def rows(base, count):
        return jnp.concatenate(
            [flat_ref[pl.ds(base + t, 24, count), :] for t in range(count)], axis=1
        )

    return rows(0, 9), rows(216, 3), rows(288, 12), [rows(576 + 72 * j, 3) for j in range(4)]


def kinds_of(top, low):
    inputs, mixing = top[:24], top[24:, :384]
    expand = jnp.concatenate([low[:24], low[24:, :384]], axis=1)
    reduces = [top[24:, 384:768], top[24:, 768:], low[24:, 384:768], low[24:, 768:]]
    return inputs, mixing, expand, reduces


def halves_of(inputs, mixing, expand, reduces):
    top = jnp.concatenate(
        [inputs, jnp.concatenate([mixing, reduces[0], reduces[1]], axis=1)], axis=0
    )
    low = jnp.concatenate(
        [
            expand[:, :1152],
            jnp.concatenate([expand[:, 1152:], reduces[2], reduces[3]], axis=1),
        ],
        axis=0,
    )
    return top, low


def kernel(
    din_h, dmix_h, dexp_h, dred_h, w_h, m_h, de_h, eo_h, em_h, basis_h,
    fin_h, fmix_h, fexp_h, fred_h, wn_h, mn_h, fe_h, ne_h, nem_h,
    din, dmix, dexp, dred, w, m, de, eo, em, basis,
    fin, fmix, fexp, fred, wn, mn, fe, ne, nem,
    rs_send, rs_mid, rs_merge, rs_recv,
    a1_send, a1_recv, a2_send, a2_recv, flat, ag,
    coef, cf_send, cf_mid, cf_merge, cf_recv, tp_send, tp_recv, stage,
    in_sem, out_sem, z_send, z_recv, a1_ss, a1_rs, a2_ss, a2_rs, tp_ss, tp_rs,
):
    r, s, t = lax.axis_index("rep"), lax.axis_index("shard"), lax.axis_index("tp")
    right, left, opp = (r + 1) % GROUPS, (r + 3) % GROUPS, (r + 2) % GROUPS

    ins = [
        pltpu.make_async_copy(a, b, in_sem.at[i])
        for i, (a, b) in enumerate(
            [(din_h, din), (dmix_h, dmix), (dexp_h, dexp), (dred_h, dred), (basis_h, basis),
             (de_h, de), (em_h, em), (eo_h.at[:, 0, :], eo), (w_h, w), (m_h, m)]
        )
    ]
    for c in ins:
        c.start()

    barrier = pltpu.get_barrier_semaphore()
    for z in (right, left):
        pl.semaphore_signal(barrier, inc=1, device_id={"rep": z}, device_id_type=MESH)
    for d in range(1, PEERS):
        pl.semaphore_signal(
            barrier, inc=1, device_id={"shard": (s + d) % PEERS}, device_id_type=MESH
        )
    pl.semaphore_signal(barrier, inc=1, device_id={"tp": 1 - t}, device_id_type=MESH)

    count = [0]

    def z_copy(src, dst, to):
        i = count[0]
        count[0] += 1
        return pltpu.make_async_remote_copy(
            src_ref=src, dst_ref=dst, send_sem=z_send.at[i], recv_sem=z_recv.at[i],
            device_id={"rep": to}, device_id_type=MESH,
        )

    for c in ins[:4]:
        c.wait()

    def pack(q, ref):
        return jnp.concatenate(
            [ref[l].astype(F32)[12 * q : 12 * q + 12] for l in range(2)], axis=0
        )

    for q in range(GROUPS):
        red = [dred[l, pl.ds(48 * q, 48), :].astype(F32) for l in range(2)]
        top, low = halves_of(
            pack(q, din), pack(q, dmix), pack(q, dexp),
            [red[0][:24], red[0][24:], red[1][:24], red[1][24:]],
        )
        rs_send[q, 0] = top.astype(BF16)
        rs_send[q, 1] = low.astype(BF16)

    pl.semaphore_wait(barrier, PEERS + 2)
    rs1 = [z_copy(rs_send.at[opp, 0], rs_mid.at[0], right),
           z_copy(rs_send.at[opp, 1], rs_mid.at[1], left)]
    for c in rs1:
        c.start()

    ins[4].wait()
    b = basis[...]
    b_hi = b.astype(BF16)
    b_lo = (b - b_hi.astype(F32)).astype(BF16)
    rhs = jnp.concatenate([b_hi, b_hi, b_lo, b_lo], axis=0)
    across = (((1,), (1,)), ((), ()))
    ins[5].wait()

    def terms(start, rows):
        y = lax.dot_general(
            de[pl.ds(start, rows), :], rhs, across, preferred_element_type=F32
        )
        coef[pl.ds(start, rows), :] = y[:, :128] + y[:, 128:]

    def body(i, carry):
        terms(pl.multiple_of(i * CHUNK, CHUNK), CHUNK)
        return carry

    lax.fori_loop(0, VROWS // CHUNK, body, 0)
    terms(VROWS // CHUNK * CHUNK, VROWS % CHUNK)
    coef[pl.ds(VROWS, 56), :] = jnp.zeros((56, 128), F32)
    lane = lanes(PACK)
    for q in range(GROUPS):
        packed = jnp.where(
            lane < RANK, coef[pl.ds(ROWS * q, PACK), :], coef[pl.ds(ROWS * q + PACK, PACK), :]
        ).astype(BF16)
        cf_send[q, 0] = packed[:HALF]
        cf_send[q, 1] = packed[HALF:]
    cf1 = [z_copy(cf_send.at[opp, 0], cf_mid.at[0], right),
           z_copy(cf_send.at[opp, 1], cf_mid.at[1], left)]
    cf2 = [z_copy(cf_send.at[right, 1], cf_recv.at[1], right),
           z_copy(cf_send.at[left, 0], cf_recv.at[3], left)]
    rs2 = [z_copy(rs_send.at[right, 1], rs_recv.at[1], right),
           z_copy(rs_send.at[left, 0], rs_recv.at[3], left)]
    for c in cf1 + cf2:
        c.start()

    for c in cf1:
        c.wait_recv()
    cf_merge[0] = (cf_send[right, 0].astype(F32) + cf_mid[0].astype(F32)).astype(BF16)
    cf_merge[1] = (cf_send[left, 1].astype(F32) + cf_mid[1].astype(F32)).astype(BF16)
    cf3 = [z_copy(cf_merge.at[0], cf_recv.at[0], right),
           z_copy(cf_merge.at[1], cf_recv.at[2], left)]
    for c in cf3 + rs2:
        c.start()

    for c in rs1:
        c.wait_recv()
    rs_merge[0] = (rs_send[right, 0].astype(F32) + rs_mid[0].astype(F32)).astype(BF16)
    rs_merge[1] = (rs_send[left, 1].astype(F32) + rs_mid[1].astype(F32)).astype(BF16)
    rs3 = [z_copy(rs_merge.at[0], rs_recv.at[0], right),
           z_copy(rs_merge.at[1], rs_recv.at[2], left)]
    for c in rs3:
        c.start()

    def total(send, recv, half):
        near, far = (recv[0], recv[3]) if half == 0 else (recv[1], recv[2])
        return send[r, half].astype(F32) + (near.astype(F32) + far.astype(F32))

    tp = []
    for half, arrived in enumerate(([cf2[1], cf3[0]], [cf2[0], cf3[1]])):
        for c in arrived:
            c.wait_recv()
        tp_send[half] = total(cf_send, cf_recv, half).astype(BF16)
        tp.append(pltpu.make_async_remote_copy(
            src_ref=tp_send.at[half], dst_ref=tp_recv.at[half],
            send_sem=tp_ss.at[half], recv_sem=tp_rs.at[half],
            device_id={"tp": 1 - t}, device_id_type=MESH,
        ))
        tp[half].start()

    for c in ins[6:8]:
        c.wait()
    momenta = jnp.transpose(em[...])
    halves = (pl.ds(0, 2 * HALF), pl.ds(2 * HALF, STAGE - 2 * HALF))
    kept, eg1, eg2 = {}, [], []
    for half, pieces in enumerate(
        (((0, 0, HALF), (2 * HALF, HALF, HALF)),
         ((HALF, 2 * HALF, HALF), (3 * HALF, 3 * HALF, ROWS - 3 * HALF)))
    ):
        tp[half].wait_recv()
        both = (tp_send[half].astype(F32) + tp_recv[half].astype(F32)) * 0.25
        for (start, at, rows), c in zip(pieces, (both, turn(both, RANK))):
            c = c[:rows, :RANK]
            momentum = MOMENTUM * momenta[start : start + rows] + c
            kept[start] = momentum
            direction = c + MOMENTUM * momentum
            d_hi = direction.astype(BF16)
            d_lo = (direction - d_hi.astype(F32)).astype(BF16)
            update = jnp.dot(d_hi, b_hi, preferred_element_type=F32)
            update += jnp.dot(d_lo, b_hi, preferred_element_type=F32)
            update += jnp.dot(d_hi, b_lo, preferred_element_type=F32)
            parts = []
            for j in range(WIDTH // 128):
                place_of = pl.ds(3 * start + j, rows, 3)
                table = eo[place_of, :] - OUTER_RATE * tile(update, j)
                ne[place_of, :] = table
                parts.append(table.astype(BF16))
            stage[r, pl.ds(at, rows), :] = jnp.concatenate(parts, axis=1)
        block = halves[half]
        far, near = (right, left) if half == 0 else (left, right)
        eg1.append(z_copy(stage.at[r, block], stage.at[r, block], far))
        eg2.append(z_copy(stage.at[r, block], stage.at[r, block], near))
        eg1[half].start()
        eg2[half].start()

    def exchange(send, recv, send_sem, recv_sem):
        copies = [
            pltpu.make_async_remote_copy(
                src_ref=send.at[(s + d) % PEERS], dst_ref=recv.at[s],
                send_sem=send_sem.at[d], recv_sem=recv_sem.at[d],
                device_id={"shard": (s + d) % PEERS}, device_id_type=MESH,
            )
            for d in range(1, PEERS)
        ]
        for c in copies:
            c.start()
        recv[s] = send[s]
        return copies

    for c in rs2 + rs3:
        c.wait_recv()
    top, low = total(rs_send, rs_recv, 0), total(rs_send, rs_recv, 1)
    split_columns(kinds_of(top * 0.25, low * 0.25), a1_send)
    a1 = exchange(a1_send, a1_recv, a1_ss, a1_rs)

    nem[...] = jnp.transpose(jnp.concatenate([kept[k] for k in sorted(kept)], axis=0))
    outs = [pltpu.make_async_copy(a, o, out_sem.at[i])
            for i, (a, o) in enumerate([(nem, nem_h), (ne, ne_h), (mn, mn_h), (wn, wn_h),
                                        (fin, fin_h), (fmix, fmix_h), (fexp, fexp_h),
                                        (fred, fred_h), (fe, fe_h)])]
    for c in outs[:2]:
        c.start()

    for c in ins[8:10]:
        c.wait()
    for c in a1:
        c.wait_recv()
    to_flat(merge_columns(a1_recv), flat)
    gradient = flat[...]
    momentum = MOMENTUM * m[...] + gradient
    mn[...] = momentum
    wn[...] = w[...] - OUTER_RATE * (gradient + MOMENTUM * momentum)
    split_columns(from_flat(wn), a2_send)
    a2 = exchange(a2_send, a2_recv, a2_ss, a2_rs)
    for c in outs[2:4]:
        c.start()
    for c in eg1:
        c.wait_recv()
    eg3 = [z_copy(stage.at[left, halves[0]], stage.at[left, halves[0]], right),
           z_copy(stage.at[right, halves[1]], stage.at[right, halves[1]], left)]
    for c in eg3:
        c.start()

    for c in a2:
        c.wait_recv()
    inputs, mixing, expand, reduces = merge_columns(a2_recv)
    join = lambda tiles: jnp.concatenate(tiles, axis=1)
    top, low = halves_of(join(inputs), join(mixing), join(expand), [join(x) for x in reduces])
    ag[r, 0] = top.astype(BF16)
    ag[r, 1] = low.astype(BF16)
    dg1 = [z_copy(ag.at[r, 0], ag.at[r, 0], right), z_copy(ag.at[r, 1], ag.at[r, 1], left)]
    dg2 = [z_copy(ag.at[r, 1], ag.at[r, 1], right), z_copy(ag.at[r, 0], ag.at[r, 0], left)]
    for c in dg1 + dg2:
        c.start()

    for c in dg1:
        c.wait_recv()
    dg3 = [z_copy(ag.at[left, 0], ag.at[left, 0], right),
           z_copy(ag.at[right, 1], ag.at[right, 1], left)]
    for c in dg3:
        c.start()

    def assemble(q):
        for to, at, rows in (
            (0, 0, HALF), (HALF, 2 * HALF, HALF), (2 * HALF, HALF, HALF),
            (3 * HALF, 3 * HALF, ROWS - 3 * HALF),
        ):
            fe[pl.ds(ROWS * q + to, rows), :] = stage[q, pl.ds(at, rows), :]

    for c in eg2:
        c.wait_recv()
    for q in range(GROUPS):
        pl.when(q != opp)(lambda q=q: assemble(q))
    for c in eg3:
        c.wait_recv()
    for q in range(GROUPS):
        pl.when(q == opp)(lambda q=q: assemble(q))
    outs[8].start()

    for c in dg2 + dg3:
        c.wait_recv()
    parts = [kinds_of(ag[q, 0].astype(F32), ag[q, 1].astype(F32)) for q in range(GROUPS)]
    for l in range(2):
        for k, out in enumerate((fin, fmix, fexp)):
            out[l] = jnp.concatenate(
                [parts[q][k][12 * l : 12 * l + 12] for q in range(GROUPS)], axis=0
            ).astype(BF16)
        for q in range(GROUPS):
            fred[l, pl.ds(48 * q, 48), :] = jnp.concatenate(
                [parts[q][3][2 * l], parts[q][3][2 * l + 1]], axis=0
            ).astype(BF16)
    for c in outs[4:8]:
        c.start()

    for c in (rs1 + rs2 + rs3 + cf1 + cf2 + cf3 + tp + a1 + a2 + eg1 + eg2 + eg3
              + dg1 + dg2 + dg3):
        c.wait_send()
    for c in outs:
        c.wait()


def flush(*refs):
    sem = refs[18]
    copies = []
    for i in range(9):
        to = refs[9 + i].at[:, 0, :] if i == 7 else refs[9 + i]
        copies.append(pltpu.make_async_copy(refs[i], to, sem.at[i]))
    for c in copies:
        c.start()
    for c in copies:
        c.wait()


def local(
    delta_inputs, delta_mixing, delta_expand, delta_reduce, owner_weights, owner_momentum,
    delta_embed, embed_owner, embed_momentum, basis,
):
    args = (
        delta_inputs[0], delta_mixing[0], delta_expand[0], delta_reduce[0],
        owner_weights.reshape(FLAT_ROWS, 128), owner_momentum.reshape(FLAT_ROWS, 128),
        delta_embed[0],
        jnp.transpose(embed_owner[0], (1, 0, 2)).reshape(3 * ROWS, 1, 128),
        embed_momentum[0, 0].T, basis.T,
    )
    table = jax.ShapeDtypeStruct((3 * ROWS, 128), F32)
    outs = args[:7] + (table, args[8])
    vmem = lambda x: pltpu.VMEM(x.shape, x.dtype)
    dma = pltpu.SemaphoreType.DMA
    half = (48, 1152)
    args = tuple(pltpu.with_memory_space_constraint(x, pltpu.HBM) for x in args)
    results = pl.pallas_call(
        kernel,
        name="outer_step",
        out_shape=[jax.ShapeDtypeStruct(x.shape, x.dtype) for x in outs],
        in_specs=[pl.BlockSpec(memory_space=pltpu.HBM)] * 10,
        out_specs=[pl.BlockSpec(memory_space=pl.ANY)] * 9,
        scratch_shapes=[vmem(x) for x in args[:7] + (table,) + args[8:]]
        + [vmem(x) for x in outs]
        + [
            pltpu.VMEM((GROUPS, 2) + half, BF16),
            pltpu.VMEM((2,) + half, BF16),
            pltpu.VMEM((2,) + half, BF16),
            pltpu.VMEM((4,) + half, BF16),
            pltpu.VMEM((PEERS, 24, 384), BF16),
            pltpu.VMEM((PEERS, 24, 384), BF16),
            pltpu.VMEM((PEERS, 24, 384), BF16),
            pltpu.VMEM((PEERS, 24, 384), BF16),
            pltpu.VMEM((FLAT_ROWS, 128), F32),
            pltpu.VMEM((GROUPS, 2) + half, BF16),
            pltpu.VMEM((VROWS + 56, 128), F32),
            pltpu.VMEM((GROUPS, 2, HALF, 128), BF16),
            pltpu.VMEM((2, HALF, 128), BF16),
            pltpu.VMEM((2, HALF, 128), BF16),
            pltpu.VMEM((4, HALF, 128), BF16),
            pltpu.VMEM((2, HALF, 128), BF16),
            pltpu.VMEM((2, HALF, 128), BF16),
            pltpu.VMEM((GROUPS, STAGE, WIDTH), BF16),
            dma((10,)),
            dma((9,)),
            dma((24,)),
            dma((24,)),
            dma((PEERS,)),
            dma((PEERS,)),
            dma((PEERS,)),
            dma((PEERS,)),
            dma((2,)),
            dma((2,)),
        ],
        compiler_params=pltpu.CompilerParams(
            collective_id=0, has_side_effects=True, vmem_limit_bytes=26 * 1024 * 1024
        ),
    )(*args)
    results = pl.pallas_call(
        flush,
        name="flush",
        out_shape=[jax.ShapeDtypeStruct(x.shape, x.dtype) for x in args[:9]],
        in_specs=[pl.BlockSpec(memory_space=pl.ANY)] * 9,
        out_specs=[pl.BlockSpec(memory_space=pl.ANY)] * 9,
        scratch_shapes=[dma((9,))],
        compiler_params=pltpu.CompilerParams(vmem_limit_bytes=1024 * 1024),
    )(*results)
    return (
        results[0], results[1], results[2], results[3],
        results[4].reshape(owner_weights.shape), results[5].reshape(owner_momentum.shape),
        results[6],
        jnp.transpose(results[7].reshape(ROWS, 1, WIDTH), (1, 0, 2))[None],
        results[8].T[None, None],
    )


def solution(mesh):
    in_specs = (
        P("rep", None, "shard", "tp"),
        P("rep", None, "shard", "tp"),
        P("rep", None, "shard", "tp"),
        P("rep", None, "shard", "tp"),
        P("rep", "shard", "tp", None),
        P("rep", "shard", "tp", None),
        P("rep", "shard", "tp"),
        P("shard", "rep", None, "tp"),
        P("shard", "rep", None, None),
        P("tp", None),
    )
    out_specs = (
        P(None, "shard", "tp"),
        P(None, "shard", "tp"),
        P(None, "shard", "tp"),
        P(None, "shard", "tp"),
        P("rep", "shard", "tp", None),
        P("rep", "shard", "tp", None),
        P("shard", "tp"),
        P("shard", "rep", None, "tp"),
        P("shard", "rep", None, None),
    )
    return jax.shard_map(local, mesh=mesh, in_specs=in_specs, out_specs=out_specs, check_vma=False)
```

```python
import jax
import jax.numpy as jnp
from jax import lax
from jax.experimental import pallas as pl
from jax.experimental.pallas import tpu as pltpu
from jax.sharding import PartitionSpec as P

MOMENTUM = 0.5
OUTER_RATE = 0.7
MESH = pl.DeviceIdType.MESH
F32 = jnp.float32
BF16 = jnp.bfloat16

GROUPS = 4
PEERS = 16
ROWS = 786
VROWS = 3144
WIDTH = 384
RANK = 64
FLAT_ROWS = 864
PACK = 416
HALF = 208
STAGE = 800
SPAN = 808
OVER = 48

W_IN, W_MIX, W_EXP, W_RED = 72, 24, 96, 24


def lanes(rows):
    return lax.broadcasted_iota(jnp.int32, (rows, 128), 1)


def tile(x, index):
    return x[:, index * 128 : (index + 1) * 128]


def turn(x, shift):
    shift = shift % 128
    return x if shift == 0 else pltpu.roll(x, shift, 1)


def place(total, lane, x, low, high):
    if total is None:
        return x
    return jnp.where((lane >= low) & (lane < high), x, total)


def piece(total, lane, src, start, width, to):
    first, last = start // 128, (start + width - 1) // 128
    shift = to - start % 128
    cut = width if first == last else last * 128 - start
    total = place(total, lane, turn(tile(src, first), shift), to, to + cut)
    if first != last:
        total = place(total, lane, turn(tile(src, last), shift), to + cut, to + width)
    return total


def split_columns(kinds, send_ref):
    inputs, mixing, expand, reduces = kinds
    lane = lanes(24)
    for u in range(PEERS):
        a = piece(None, lane, inputs, u * W_IN, W_IN, 0)
        a = piece(a, lane, mixing, u * W_MIX, W_MIX, W_IN)
        b = piece(None, lane, expand, u * W_EXP, W_EXP, 0)
        c = None
        for j in range(4):
            c = piece(c, lane, reduces[j], u * W_RED, W_RED, j * W_RED)
        send_ref[u] = jnp.concatenate([a, b, c], axis=1).astype(BF16)


def merge_columns(recv_ref):
    lane = lanes(24)
    blocks = [recv_ref[s].astype(F32) for s in range(PEERS)]

    def kind(which, width, base):
        out = []
        for t in range(PEERS * width // 128):
            total = None
            for s in range(PEERS):
                low, high = max(s * width - t * 128, 0), min((s + 1) * width - t * 128, 128)
                if low >= high:
                    continue
                shifted = turn(tile(blocks[s], which), s * width - t * 128 - base)
                total = place(total, lane, shifted, low, high)
            out.append(total)
        return out

    return (
        kind(0, W_IN, 0),
        kind(0, W_MIX, W_IN),
        kind(1, W_EXP, 0),
        [kind(2, W_RED, j * W_RED) for j in range(4)],
    )


def to_flat(kinds, flat_ref):
    inputs, mixing, expand, reduces = kinds
    for base, tiles in (
        [(0, inputs), (216, mixing), (288, expand)] + [(576 + 72 * j, reduces[j]) for j in range(4)]
    ):
        count = len(tiles)
        for t in range(count):
            flat_ref[pl.ds(base + t, 24, count), :] = tiles[t]


def from_flat(flat_ref):
    def rows(base, count):
        return jnp.concatenate(
            [flat_ref[pl.ds(base + t, 24, count), :] for t in range(count)], axis=1
        )

    return rows(0, 9), rows(216, 3), rows(288, 12), [rows(576 + 72 * j, 3) for j in range(4)]


def kinds_of(top, low):
    inputs, mixing = top[:24], top[24:, :384]
    expand = jnp.concatenate([low[:24], low[24:, :384]], axis=1)
    reduces = [top[24:, 384:768], top[24:, 768:], low[24:, 384:768], low[24:, 768:]]
    return inputs, mixing, expand, reduces


def halves_of(inputs, mixing, expand, reduces):
    top = jnp.concatenate(
        [inputs, jnp.concatenate([mixing, reduces[0], reduces[1]], axis=1)], axis=0
    )
    low = jnp.concatenate(
        [
            expand[:, :1152],
            jnp.concatenate([expand[:, 1152:], reduces[2], reduces[3]], axis=1),
        ],
        axis=0,
    )
    return top, low


def kernel(
    din_h, dmix_h, dexp_h, dred_h, w_h, m_h, de_h, eo_h, em_h, basis_h,
    fin_h, fmix_h, fexp_h, fred_h, wn_h, mn_h, fe_h, ne_h, nem_h,
    din, dmix, dexp, dred, w, m, de, eo, em, basis,
    fin, fmix, fexp, fred, wn, mn, fe, ne, nem,
    rs_send, rs_mid, rs_merge, rs_recv,
    a1_send, a1_recv, a2_send, a2_recv, flat, ag,
    coef, cf_send, cf_mid, cf_merge, cf_recv, tp_send, tp_recv, stage,
    in_sem, out_sem, z_send, z_recv, a1_ss, a1_rs, a2_ss, a2_rs, tp_ss, tp_rs,
):
    r, s, t = lax.axis_index("rep"), lax.axis_index("shard"), lax.axis_index("tp")
    right, left, opp = (r + 1) % GROUPS, (r + 3) % GROUPS, (r + 2) % GROUPS

    ins = [
        pltpu.make_async_copy(a, b, in_sem.at[i])
        for i, (a, b) in enumerate(
            [(basis_h, basis), (de_h, de), (din_h, din), (dmix_h, dmix), (dexp_h, dexp),
             (dred_h, dred), (em_h, em), (eo_h.at[:, 0, :], eo), (w_h, w), (m_h, m)]
        )
    ]
    for c in ins:
        c.start()

    barrier = pltpu.get_barrier_semaphore()
    for z in (right, left):
        pl.semaphore_signal(barrier, inc=1, device_id={"rep": z}, device_id_type=MESH)
    for d in range(1, PEERS):
        pl.semaphore_signal(
            barrier, inc=1, device_id={"shard": (s + d) % PEERS}, device_id_type=MESH
        )
    pl.semaphore_signal(barrier, inc=1, device_id={"tp": 1 - t}, device_id_type=MESH)

    count = [0]

    def z_copy(src, dst, to):
        i = count[0]
        count[0] += 1
        return pltpu.make_async_remote_copy(
            src_ref=src, dst_ref=dst, send_sem=z_send.at[i], recv_sem=z_recv.at[i],
            device_id={"rep": to}, device_id_type=MESH,
        )

    ins[0].wait()
    b = basis[...]
    b_hi = b.astype(BF16)
    b_lo = (b - b_hi.astype(F32)).astype(BF16)
    rhs = jnp.concatenate([b_hi, b_hi, b_lo, b_lo], axis=0)
    across = (((1,), (1,)), ((), ()))
    lane = lanes(PACK)
    for k in range(GROUPS):
        coef[k, pl.ds(SPAN, OVER), :] = jnp.zeros((OVER, 128), F32)
    ins[1].wait()

    def terms(k, q):
        start = pl.multiple_of(784 * q - 16 * (q // 3), 16)
        for at, rows in ((0, 400), (400, SPAN - 400)):
            y = lax.dot_general(
                de[pl.ds(start + at, rows), :], rhs, across, preferred_element_type=F32
            )
            coef[k, pl.ds(at, rows), :] = y[:, :128] + y[:, 128:]
        skip = 2 * q + 16 * (q // 3)
        packed = jnp.where(
            lane < RANK, coef[k, pl.ds(skip, PACK), :], coef[k, pl.ds(skip + PACK, PACK), :]
        ).astype(BF16)
        cf_send[q, 0] = packed[:HALF]
        cf_send[q, 1] = packed[HALF:]

    terms(0, opp)
    pl.semaphore_wait(barrier, PEERS + 2)
    cf1 = [z_copy(cf_send.at[opp, 0], cf_mid.at[0], right),
           z_copy(cf_send.at[opp, 1], cf_mid.at[1], left)]
    for c in cf1:
        c.start()
    terms(1, right)
    terms(2, left)
    cf2 = [z_copy(cf_send.at[right, 1], cf_recv.at[1], right),
           z_copy(cf_send.at[left, 0], cf_recv.at[3], left)]
    for c in cf2:
        c.start()

    for c in ins[2:6]:
        c.wait()

    def pack(q, ref):
        return jnp.concatenate(
            [ref[l].astype(F32)[12 * q : 12 * q + 12] for l in range(2)], axis=0
        )

    for q in range(GROUPS):
        red = [dred[l, pl.ds(48 * q, 48), :].astype(F32) for l in range(2)]
        top, low = halves_of(
            pack(q, din), pack(q, dmix), pack(q, dexp),
            [red[0][:24], red[0][24:], red[1][:24], red[1][24:]],
        )
        rs_send[q, 0] = top.astype(BF16)
        rs_send[q, 1] = low.astype(BF16)

    rs1 = [z_copy(rs_send.at[opp, 0], rs_mid.at[0], right),
           z_copy(rs_send.at[opp, 1], rs_mid.at[1], left)]
    for c in rs1:
        c.start()

    terms(3, r)
    rs2 = [z_copy(rs_send.at[right, 1], rs_recv.at[1], right),
           z_copy(rs_send.at[left, 0], rs_recv.at[3], left)]

    for c in cf1:
        c.wait_recv()
    cf_merge[0] = (cf_send[right, 0].astype(F32) + cf_mid[0].astype(F32)).astype(BF16)
    cf_merge[1] = (cf_send[left, 1].astype(F32) + cf_mid[1].astype(F32)).astype(BF16)
    cf3 = [z_copy(cf_merge.at[0], cf_recv.at[0], right),
           z_copy(cf_merge.at[1], cf_recv.at[2], left)]
    for c in cf3 + rs2:
        c.start()

    for c in rs1:
        c.wait_recv()
    rs_merge[0] = (rs_send[right, 0].astype(F32) + rs_mid[0].astype(F32)).astype(BF16)
    rs_merge[1] = (rs_send[left, 1].astype(F32) + rs_mid[1].astype(F32)).astype(BF16)
    rs3 = [z_copy(rs_merge.at[0], rs_recv.at[0], right),
           z_copy(rs_merge.at[1], rs_recv.at[2], left)]
    for c in rs3:
        c.start()

    def total(send, recv, half):
        near, far = (recv[0], recv[3]) if half == 0 else (recv[1], recv[2])
        return send[r, half].astype(F32) + (near.astype(F32) + far.astype(F32))

    tp = []
    for half, arrived in enumerate(([cf2[1], cf3[0]], [cf2[0], cf3[1]])):
        for c in arrived:
            c.wait_recv()
        tp_send[half] = total(cf_send, cf_recv, half).astype(BF16)
        tp.append(pltpu.make_async_remote_copy(
            src_ref=tp_send.at[half], dst_ref=tp_recv.at[half],
            send_sem=tp_ss.at[half], recv_sem=tp_rs.at[half],
            device_id={"tp": 1 - t}, device_id_type=MESH,
        ))
        tp[half].start()

    for c in ins[6:8]:
        c.wait()
    momenta = jnp.transpose(em[...])
    halves = (pl.ds(0, 2 * HALF), pl.ds(2 * HALF, STAGE - 2 * HALF))
    kept, eg1, eg2 = {}, [], []
    for half, pieces in enumerate(
        (((0, 0, HALF), (2 * HALF, HALF, HALF)),
         ((HALF, 2 * HALF, HALF), (3 * HALF, 3 * HALF, ROWS - 3 * HALF)))
    ):
        tp[half].wait_recv()
        both = (tp_send[half].astype(F32) + tp_recv[half].astype(F32)) * 0.25
        for (start, at, rows), c in zip(pieces, (both, turn(both, RANK))):
            c = c[:rows, :RANK]
            momentum = MOMENTUM * momenta[start : start + rows] + c
            kept[start] = momentum
            direction = c + MOMENTUM * momentum
            d_hi = direction.astype(BF16)
            d_lo = (direction - d_hi.astype(F32)).astype(BF16)
            update = jnp.dot(d_hi, b_hi, preferred_element_type=F32)
            update += jnp.dot(d_lo, b_hi, preferred_element_type=F32)
            update += jnp.dot(d_hi, b_lo, preferred_element_type=F32)
            parts = []
            for j in range(WIDTH // 128):
                place_of = pl.ds(3 * start + j, rows, 3)
                table = eo[place_of, :] - OUTER_RATE * tile(update, j)
                ne[place_of, :] = table
                parts.append(table.astype(BF16))
            stage[r, pl.ds(at, rows), :] = jnp.concatenate(parts, axis=1)
        block = halves[half]
        far, near = (right, left) if half == 0 else (left, right)
        eg1.append(z_copy(stage.at[r, block], stage.at[r, block], far))
        eg2.append(z_copy(stage.at[r, block], stage.at[r, block], near))
        eg1[half].start()
        eg2[half].start()

    def exchange(send, recv, send_sem, recv_sem):
        copies = [
            pltpu.make_async_remote_copy(
                src_ref=send.at[(s + d) % PEERS], dst_ref=recv.at[s],
                send_sem=send_sem.at[d], recv_sem=recv_sem.at[d],
                device_id={"shard": (s + d) % PEERS}, device_id_type=MESH,
            )
            for d in range(1, PEERS)
        ]
        for c in copies:
            c.start()
        recv[s] = send[s]
        return copies

    for c in rs2 + rs3:
        c.wait_recv()
    top, low = total(rs_send, rs_recv, 0), total(rs_send, rs_recv, 1)
    split_columns(kinds_of(top * 0.25, low * 0.25), a1_send)
    a1 = exchange(a1_send, a1_recv, a1_ss, a1_rs)

    nem[...] = jnp.transpose(jnp.concatenate([kept[k] for k in sorted(kept)], axis=0))
    outs = [pltpu.make_async_copy(a, o, out_sem.at[i])
            for i, (a, o) in enumerate([(nem, nem_h), (ne, ne_h), (mn, mn_h), (wn, wn_h),
                                        (fin, fin_h), (fmix, fmix_h), (fexp, fexp_h),
                                        (fred, fred_h), (fe, fe_h)])]
    for c in outs[:2]:
        c.start()

    for c in ins[8:10]:
        c.wait()
    for c in a1:
        c.wait_recv()
    to_flat(merge_columns(a1_recv), flat)
    gradient = flat[...]
    momentum = MOMENTUM * m[...] + gradient
    mn[...] = momentum
    wn[...] = w[...] - OUTER_RATE * (gradient + MOMENTUM * momentum)
    split_columns(from_flat(wn), a2_send)
    a2 = exchange(a2_send, a2_recv, a2_ss, a2_rs)
    for c in outs[2:4]:
        c.start()
    for c in eg1:
        c.wait_recv()
    eg3 = [z_copy(stage.at[left, halves[0]], stage.at[left, halves[0]], right),
           z_copy(stage.at[right, halves[1]], stage.at[right, halves[1]], left)]
    for c in eg3:
        c.start()

    for c in a2:
        c.wait_recv()
    inputs, mixing, expand, reduces = merge_columns(a2_recv)
    join = lambda tiles: jnp.concatenate(tiles, axis=1)
    top, low = halves_of(join(inputs), join(mixing), join(expand), [join(x) for x in reduces])
    ag[r, 0] = top.astype(BF16)
    ag[r, 1] = low.astype(BF16)
    dg1 = [z_copy(ag.at[r, 0], ag.at[r, 0], right), z_copy(ag.at[r, 1], ag.at[r, 1], left)]
    dg2 = [z_copy(ag.at[r, 1], ag.at[r, 1], right), z_copy(ag.at[r, 0], ag.at[r, 0], left)]
    for c in dg1 + dg2:
        c.start()

    for c in dg1:
        c.wait_recv()
    dg3 = [z_copy(ag.at[left, 0], ag.at[left, 0], right),
           z_copy(ag.at[right, 1], ag.at[right, 1], left)]
    for c in dg3:
        c.start()

    def assemble(q):
        for to, at, rows in (
            (0, 0, HALF), (HALF, 2 * HALF, HALF), (2 * HALF, HALF, HALF),
            (3 * HALF, 3 * HALF, ROWS - 3 * HALF),
        ):
            fe[pl.ds(ROWS * q + to, rows), :] = stage[q, pl.ds(at, rows), :]

    for c in eg2:
        c.wait_recv()
    for q in range(GROUPS):
        pl.when(q != opp)(lambda q=q: assemble(q))
    for c in eg3:
        c.wait_recv()
    for q in range(GROUPS):
        pl.when(q == opp)(lambda q=q: assemble(q))
    outs[8].start()

    for c in dg2 + dg3:
        c.wait_recv()
    parts = [kinds_of(ag[q, 0].astype(F32), ag[q, 1].astype(F32)) for q in range(GROUPS)]
    for l in range(2):
        for k, out in enumerate((fin, fmix, fexp)):
            out[l] = jnp.concatenate(
                [parts[q][k][12 * l : 12 * l + 12] for q in range(GROUPS)], axis=0
            ).astype(BF16)
        for q in range(GROUPS):
            fred[l, pl.ds(48 * q, 48), :] = jnp.concatenate(
                [parts[q][3][2 * l], parts[q][3][2 * l + 1]], axis=0
            ).astype(BF16)
    for c in outs[4:8]:
        c.start()

    for c in (rs1 + rs2 + rs3 + cf1 + cf2 + cf3 + tp + a1 + a2 + eg1 + eg2 + eg3
              + dg1 + dg2 + dg3):
        c.wait_send()
    for c in outs:
        c.wait()


def flush(*refs):
    sem = refs[18]
    copies = []
    for i in range(9):
        to = refs[9 + i].at[:, 0, :] if i == 7 else refs[9 + i]
        copies.append(pltpu.make_async_copy(refs[i], to, sem.at[i]))
    for c in copies:
        c.start()
    for c in copies:
        c.wait()


def local(
    delta_inputs, delta_mixing, delta_expand, delta_reduce, owner_weights, owner_momentum,
    delta_embed, embed_owner, embed_momentum, basis,
):
    args = (
        delta_inputs[0], delta_mixing[0], delta_expand[0], delta_reduce[0],
        owner_weights.reshape(FLAT_ROWS, 128), owner_momentum.reshape(FLAT_ROWS, 128),
        delta_embed[0],
        jnp.transpose(embed_owner[0], (1, 0, 2)).reshape(3 * ROWS, 1, 128),
        embed_momentum[0, 0].T, basis.T,
    )
    table = jax.ShapeDtypeStruct((3 * ROWS, 128), F32)
    outs = args[:7] + (table, args[8])
    vmem = lambda x: pltpu.VMEM(x.shape, x.dtype)
    dma = pltpu.SemaphoreType.DMA
    half = (48, 1152)
    args = tuple(pltpu.with_memory_space_constraint(x, pltpu.HBM) for x in args)
    results = pl.pallas_call(
        kernel,
        name="outer_step",
        out_shape=[jax.ShapeDtypeStruct(x.shape, x.dtype) for x in outs],
        in_specs=[pl.BlockSpec(memory_space=pltpu.HBM)] * 10,
        out_specs=[pl.BlockSpec(memory_space=pl.ANY)] * 9,
        scratch_shapes=[vmem(x) for x in args[:7] + (table,) + args[8:]]
        + [vmem(x) for x in outs]
        + [
            pltpu.VMEM((GROUPS, 2) + half, BF16),
            pltpu.VMEM((2,) + half, BF16),
            pltpu.VMEM((2,) + half, BF16),
            pltpu.VMEM((4,) + half, BF16),
            pltpu.VMEM((PEERS, 24, 384), BF16),
            pltpu.VMEM((PEERS, 24, 384), BF16),
            pltpu.VMEM((PEERS, 24, 384), BF16),
            pltpu.VMEM((PEERS, 24, 384), BF16),
            pltpu.VMEM((FLAT_ROWS, 128), F32),
            pltpu.VMEM((GROUPS, 2) + half, BF16),
            pltpu.VMEM((GROUPS, SPAN + OVER, 128), F32),
            pltpu.VMEM((GROUPS, 2, HALF, 128), BF16),
            pltpu.VMEM((2, HALF, 128), BF16),
            pltpu.VMEM((2, HALF, 128), BF16),
            pltpu.VMEM((4, HALF, 128), BF16),
            pltpu.VMEM((2, HALF, 128), BF16),
            pltpu.VMEM((2, HALF, 128), BF16),
            pltpu.VMEM((GROUPS, STAGE, WIDTH), BF16),
            dma((10,)),
            dma((9,)),
            dma((24,)),
            dma((24,)),
            dma((PEERS,)),
            dma((PEERS,)),
            dma((PEERS,)),
            dma((PEERS,)),
            dma((2,)),
            dma((2,)),
        ],
        compiler_params=pltpu.CompilerParams(
            collective_id=0, has_side_effects=True, vmem_limit_bytes=26 * 1024 * 1024
        ),
    )(*args)
    results = pl.pallas_call(
        flush,
        name="flush",
        out_shape=[jax.ShapeDtypeStruct(x.shape, x.dtype) for x in args[:9]],
        in_specs=[pl.BlockSpec(memory_space=pl.ANY)] * 9,
        out_specs=[pl.BlockSpec(memory_space=pl.ANY)] * 9,
        scratch_shapes=[dma((9,))],
        compiler_params=pltpu.CompilerParams(vmem_limit_bytes=1024 * 1024),
    )(*results)
    return (
        results[0], results[1], results[2], results[3],
        results[4].reshape(owner_weights.shape), results[5].reshape(owner_momentum.shape),
        results[6],
        jnp.transpose(results[7].reshape(ROWS, 1, WIDTH), (1, 0, 2))[None],
        results[8].T[None, None],
    )


def solution(mesh):
    in_specs = (
        P("rep", None, "shard", "tp"),
        P("rep", None, "shard", "tp"),
        P("rep", None, "shard", "tp"),
        P("rep", None, "shard", "tp"),
        P("rep", "shard", "tp", None),
        P("rep", "shard", "tp", None),
        P("rep", "shard", "tp"),
        P("shard", "rep", None, "tp"),
        P("shard", "rep", None, None),
        P("tp", None),
    )
    out_specs = (
        P(None, "shard", "tp"),
        P(None, "shard", "tp"),
        P(None, "shard", "tp"),
        P(None, "shard", "tp"),
        P("rep", "shard", "tp", None),
        P("rep", "shard", "tp", None),
        P("shard", "tp"),
        P("shard", "rep", None, "tp"),
        P("shard", "rep", None, None),
    )
    return jax.shard_map(local, mesh=mesh, in_specs=in_specs, out_specs=out_specs, check_vma=False)
```

```python
import jax
import jax.numpy as jnp
from jax import lax
from jax.experimental import pallas as pl
from jax.experimental.pallas import tpu as pltpu
from jax.sharding import PartitionSpec as P

MOMENTUM = 0.5
OUTER_RATE = 0.7
MESH = pl.DeviceIdType.MESH
F32 = jnp.float32
BF16 = jnp.bfloat16

GROUPS = 4
PEERS = 16
ROWS = 786
VROWS = 3144
WIDTH = 384
RANK = 64
FLAT_ROWS = 864
PACK = 400
HALF = 200
STAGE = 800
SPAN = 808
OVER = 48

W_IN, W_MIX, W_EXP, W_RED = 72, 24, 96, 24


def lanes(rows):
    return lax.broadcasted_iota(jnp.int32, (rows, 128), 1)


def tile(x, index):
    return x[:, index * 128 : (index + 1) * 128]


def turn(x, shift):
    shift = shift % 128
    return x if shift == 0 else pltpu.roll(x, shift, 1)


def place(total, lane, x, low, high):
    if total is None:
        return x
    return jnp.where((lane >= low) & (lane < high), x, total)


def piece(total, lane, src, start, width, to):
    first, last = start // 128, (start + width - 1) // 128
    shift = to - start % 128
    cut = width if first == last else last * 128 - start
    total = place(total, lane, turn(tile(src, first), shift), to, to + cut)
    if first != last:
        total = place(total, lane, turn(tile(src, last), shift), to + cut, to + width)
    return total


def split_columns(kinds, send_ref):
    inputs, mixing, expand, reduces = kinds
    lane = lanes(24)
    for u in range(PEERS):
        a = piece(None, lane, inputs, u * W_IN, W_IN, 0)
        a = piece(a, lane, mixing, u * W_MIX, W_MIX, W_IN)
        b = piece(None, lane, expand, u * W_EXP, W_EXP, 0)
        c = None
        for j in range(4):
            c = piece(c, lane, reduces[j], u * W_RED, W_RED, j * W_RED)
        send_ref[u] = jnp.concatenate([a, b, c], axis=1).astype(BF16)


def merge_columns(recv_ref):
    lane = lanes(24)
    blocks = [recv_ref[s].astype(F32) for s in range(PEERS)]

    def kind(which, width, base):
        out = []
        for t in range(PEERS * width // 128):
            total = None
            for s in range(PEERS):
                low, high = max(s * width - t * 128, 0), min((s + 1) * width - t * 128, 128)
                if low >= high:
                    continue
                shifted = turn(tile(blocks[s], which), s * width - t * 128 - base)
                total = place(total, lane, shifted, low, high)
            out.append(total)
        return out

    return (
        kind(0, W_IN, 0),
        kind(0, W_MIX, W_IN),
        kind(1, W_EXP, 0),
        [kind(2, W_RED, j * W_RED) for j in range(4)],
    )


def to_flat(kinds, flat_ref):
    inputs, mixing, expand, reduces = kinds
    for base, tiles in (
        [(0, inputs), (216, mixing), (288, expand)] + [(576 + 72 * j, reduces[j]) for j in range(4)]
    ):
        count = len(tiles)
        for t in range(count):
            flat_ref[pl.ds(base + t, 24, count), :] = tiles[t]


def from_flat(flat_ref):
    def rows(base, count):
        return jnp.concatenate(
            [flat_ref[pl.ds(base + t, 24, count), :] for t in range(count)], axis=1
        )

    return rows(0, 9), rows(216, 3), rows(288, 12), [rows(576 + 72 * j, 3) for j in range(4)]


def kinds_of(top, low):
    inputs, mixing = top[:24], top[24:, :384]
    expand = jnp.concatenate([low[:24], low[24:, :384]], axis=1)
    reduces = [top[24:, 384:768], top[24:, 768:], low[24:, 384:768], low[24:, 768:]]
    return inputs, mixing, expand, reduces


def halves_of(inputs, mixing, expand, reduces):
    top = jnp.concatenate(
        [inputs, jnp.concatenate([mixing, reduces[0], reduces[1]], axis=1)], axis=0
    )
    low = jnp.concatenate(
        [
            expand[:, :1152],
            jnp.concatenate([expand[:, 1152:], reduces[2], reduces[3]], axis=1),
        ],
        axis=0,
    )
    return top, low


def kernel(
    din_h, dmix_h, dexp_h, dred_h, w_h, m_h, de_h, eo_h, em_h, basis_h,
    fin_h, fmix_h, fexp_h, fred_h, wn_h, mn_h, fe_h, ne_h, nem_h,
    din, dmix, dexp, dred, w, m, de, eo, em, basis,
    fin, fmix, fexp, fred, wn, mn, fe, ne, nem,
    rs_send, rs_mid, rs_merge, rs_recv,
    a1_send, a1_recv, a2_send, a2_recv, flat, ag,
    coef, cf_send, cf_mid, cf_merge, cf_recv, tp_send, tp_recv, stage,
    in_sem, out_sem, z_send, z_recv, a1_ss, a1_rs, a2_ss, a2_rs, tp_ss, tp_rs,
):
    r, s, t = lax.axis_index("rep"), lax.axis_index("shard"), lax.axis_index("tp")
    right, left, opp = (r + 1) % GROUPS, (r + 3) % GROUPS, (r + 2) % GROUPS

    ins = [
        pltpu.make_async_copy(a, b, in_sem.at[i])
        for i, (a, b) in enumerate(
            [(basis_h, basis), (de_h, de), (din_h, din), (dmix_h, dmix), (dexp_h, dexp),
             (dred_h, dred), (em_h, em), (eo_h.at[:, 0, :], eo), (w_h, w), (m_h, m)]
        )
    ]
    for c in ins:
        c.start()

    barrier = pltpu.get_barrier_semaphore()
    for z in (right, left):
        pl.semaphore_signal(barrier, inc=1, device_id={"rep": z}, device_id_type=MESH)
    for d in range(1, PEERS):
        pl.semaphore_signal(
            barrier, inc=1, device_id={"shard": (s + d) % PEERS}, device_id_type=MESH
        )
    pl.semaphore_signal(barrier, inc=1, device_id={"tp": 1 - t}, device_id_type=MESH)

    count = [0]

    def z_copy(src, dst, to):
        i = count[0]
        count[0] += 1
        return pltpu.make_async_remote_copy(
            src_ref=src, dst_ref=dst, send_sem=z_send.at[i], recv_sem=z_recv.at[i],
            device_id={"rep": to}, device_id_type=MESH,
        )

    ins[0].wait()
    b = basis[...]
    b_hi = b.astype(BF16)
    b_lo = (b - b_hi.astype(F32)).astype(BF16)
    rhs = jnp.concatenate([b_hi, b_hi, b_lo, b_lo], axis=0)
    across = (((1,), (1,)), ((), ()))
    lane = lanes(PACK)
    for k in range(GROUPS):
        coef[k, pl.ds(SPAN, OVER), :] = jnp.zeros((OVER, 128), F32)
    ins[1].wait()

    def terms(k, q):
        start = pl.multiple_of(784 * q - 16 * (q // 3), 16)
        for at, rows in ((0, 400), (400, SPAN - 400)):
            y = lax.dot_general(
                de[pl.ds(start + at, rows), :], rhs, across, preferred_element_type=F32
            )
            coef[k, pl.ds(at, rows), :] = y[:, :128] + y[:, 128:]
        skip = 2 * q + 16 * (q // 3)
        packed = jnp.where(
            lane < RANK, coef[k, pl.ds(skip, PACK), :], coef[k, pl.ds(skip + PACK, PACK), :]
        ).astype(BF16)
        cf_send[q, 0] = packed[:HALF]
        cf_send[q, 1] = packed[HALF:]

    terms(0, opp)
    pl.semaphore_wait(barrier, PEERS + 2)
    cf1 = [z_copy(cf_send.at[opp, 0], cf_mid.at[0], right),
           z_copy(cf_send.at[opp, 1], cf_mid.at[1], left)]
    for c in cf1:
        c.start()
    terms(1, right)
    terms(2, left)
    cf2 = [z_copy(cf_send.at[right, 1], cf_recv.at[1], right),
           z_copy(cf_send.at[left, 0], cf_recv.at[3], left)]
    for c in cf2:
        c.start()

    for c in ins[2:6]:
        c.wait()

    def pack(q, ref):
        return jnp.concatenate(
            [ref[l].astype(F32)[12 * q : 12 * q + 12] for l in range(2)], axis=0
        )

    for q in range(GROUPS):
        red = [dred[l, pl.ds(48 * q, 48), :].astype(F32) for l in range(2)]
        top, low = halves_of(
            pack(q, din), pack(q, dmix), pack(q, dexp),
            [red[0][:24], red[0][24:], red[1][:24], red[1][24:]],
        )
        rs_send[q, 0] = top.astype(BF16)
        rs_send[q, 1] = low.astype(BF16)

    rs1 = [z_copy(rs_send.at[opp, 0], rs_mid.at[0], right),
           z_copy(rs_send.at[opp, 1], rs_mid.at[1], left)]
    for c in rs1:
        c.start()

    terms(3, r)
    rs2 = [z_copy(rs_send.at[right, 1], rs_recv.at[1], right),
           z_copy(rs_send.at[left, 0], rs_recv.at[3], left)]

    for c in cf1:
        c.wait_recv()
    cf_merge[0] = (cf_send[right, 0].astype(F32) + cf_mid[0].astype(F32)).astype(BF16)
    cf_merge[1] = (cf_send[left, 1].astype(F32) + cf_mid[1].astype(F32)).astype(BF16)
    cf3 = [z_copy(cf_merge.at[0], cf_recv.at[0], right),
           z_copy(cf_merge.at[1], cf_recv.at[2], left)]
    for c in cf3 + rs2:
        c.start()

    for c in rs1:
        c.wait_recv()
    rs_merge[0] = (rs_send[right, 0].astype(F32) + rs_mid[0].astype(F32)).astype(BF16)
    rs_merge[1] = (rs_send[left, 1].astype(F32) + rs_mid[1].astype(F32)).astype(BF16)
    rs3 = [z_copy(rs_merge.at[0], rs_recv.at[0], right),
           z_copy(rs_merge.at[1], rs_recv.at[2], left)]
    for c in rs3:
        c.start()

    def total(send, recv, half):
        near, far = (recv[0], recv[3]) if half == 0 else (recv[1], recv[2])
        return send[r, half].astype(F32) + (near.astype(F32) + far.astype(F32))

    tp = []
    for half, arrived in enumerate(([cf2[1], cf3[0]], [cf2[0], cf3[1]])):
        for c in arrived:
            c.wait_recv()
        tp_send[half] = total(cf_send, cf_recv, half).astype(BF16)
        tp.append(pltpu.make_async_remote_copy(
            src_ref=tp_send.at[half], dst_ref=tp_recv.at[half],
            send_sem=tp_ss.at[half], recv_sem=tp_rs.at[half],
            device_id={"tp": 1 - t}, device_id_type=MESH,
        ))
        tp[half].start()

    for c in ins[6:8]:
        c.wait()
    momenta = jnp.transpose(em[...])
    halves = (pl.ds(0, 2 * HALF), pl.ds(2 * HALF, STAGE - 2 * HALF))
    kept, eg1, eg2 = {}, [], []
    for half, pieces in enumerate(
        (((0, 0, HALF), (2 * HALF, HALF, HALF)),
         ((HALF, 2 * HALF, HALF), (3 * HALF, 3 * HALF, ROWS - 3 * HALF)))
    ):
        tp[half].wait_recv()
        both = (tp_send[half].astype(F32) + tp_recv[half].astype(F32)) * 0.25
        for (start, at, rows), c in zip(pieces, (both, turn(both, RANK))):
            c = c[:rows, :RANK]
            momentum = MOMENTUM * momenta[start : start + rows] + c
            kept[start] = momentum
            direction = c + MOMENTUM * momentum
            d_hi = direction.astype(BF16)
            d_lo = (direction - d_hi.astype(F32)).astype(BF16)
            update = jnp.dot(d_hi, b_hi, preferred_element_type=F32)
            update += jnp.dot(d_lo, b_hi, preferred_element_type=F32)
            update += jnp.dot(d_hi, b_lo, preferred_element_type=F32)
            parts = []
            for j in range(WIDTH // 128):
                place_of = pl.ds(3 * start + j, rows, 3)
                table = eo[place_of, :] - OUTER_RATE * tile(update, j)
                ne[place_of, :] = table
                parts.append(table.astype(BF16))
            stage[r, pl.ds(at, rows), :] = jnp.concatenate(parts, axis=1)
        block = halves[half]
        far, near = (right, left) if half == 0 else (left, right)
        eg1.append(z_copy(stage.at[r, block], stage.at[r, block], far))
        eg2.append(z_copy(stage.at[r, block], stage.at[r, block], near))
        eg1[half].start()
        eg2[half].start()

    def exchange(send, recv, send_sem, recv_sem):
        copies = [
            pltpu.make_async_remote_copy(
                src_ref=send.at[(s + d) % PEERS], dst_ref=recv.at[s],
                send_sem=send_sem.at[d], recv_sem=recv_sem.at[d],
                device_id={"shard": (s + d) % PEERS}, device_id_type=MESH,
            )
            for d in range(1, PEERS)
        ]
        for c in copies:
            c.start()
        recv[s] = send[s]
        return copies

    for c in rs2 + rs3:
        c.wait_recv()
    top, low = total(rs_send, rs_recv, 0), total(rs_send, rs_recv, 1)
    split_columns(kinds_of(top * 0.25, low * 0.25), a1_send)
    a1 = exchange(a1_send, a1_recv, a1_ss, a1_rs)

    nem[...] = jnp.transpose(jnp.concatenate([kept[k] for k in sorted(kept)], axis=0))
    outs = [pltpu.make_async_copy(a, o, out_sem.at[i])
            for i, (a, o) in enumerate([(nem, nem_h), (ne, ne_h), (mn, mn_h), (wn, wn_h),
                                        (fin, fin_h), (fmix, fmix_h), (fexp, fexp_h),
                                        (fred, fred_h), (fe, fe_h)])]
    for c in outs[:2]:
        c.start()

    for c in ins[8:10]:
        c.wait()
    for c in a1:
        c.wait_recv()
    to_flat(merge_columns(a1_recv), flat)
    gradient = flat[...]
    momentum = MOMENTUM * m[...] + gradient
    mn[...] = momentum
    wn[...] = w[...] - OUTER_RATE * (gradient + MOMENTUM * momentum)
    split_columns(from_flat(wn), a2_send)
    a2 = exchange(a2_send, a2_recv, a2_ss, a2_rs)
    for c in outs[2:4]:
        c.start()
    for c in eg1:
        c.wait_recv()
    eg3 = [z_copy(stage.at[left, halves[0]], stage.at[left, halves[0]], right),
           z_copy(stage.at[right, halves[1]], stage.at[right, halves[1]], left)]
    for c in eg3:
        c.start()

    for c in a2:
        c.wait_recv()
    inputs, mixing, expand, reduces = merge_columns(a2_recv)
    join = lambda tiles: jnp.concatenate(tiles, axis=1)
    top, low = halves_of(join(inputs), join(mixing), join(expand), [join(x) for x in reduces])
    ag[r, 0] = top.astype(BF16)
    ag[r, 1] = low.astype(BF16)
    dg1 = [z_copy(ag.at[r, 0], ag.at[r, 0], right), z_copy(ag.at[r, 1], ag.at[r, 1], left)]
    dg2 = [z_copy(ag.at[r, 1], ag.at[r, 1], right), z_copy(ag.at[r, 0], ag.at[r, 0], left)]
    for c in dg1 + dg2:
        c.start()

    for c in dg1:
        c.wait_recv()
    dg3 = [z_copy(ag.at[left, 0], ag.at[left, 0], right),
           z_copy(ag.at[right, 1], ag.at[right, 1], left)]
    for c in dg3:
        c.start()

    def assemble(q):
        for to, at, rows in (
            (0, 0, HALF), (HALF, 2 * HALF, HALF), (2 * HALF, HALF, HALF),
            (3 * HALF, 3 * HALF, ROWS - 3 * HALF),
        ):
            fe[pl.ds(ROWS * q + to, rows), :] = stage[q, pl.ds(at, rows), :]

    for c in eg2:
        c.wait_recv()
    for q in range(GROUPS):
        pl.when(q != opp)(lambda q=q: assemble(q))
    for c in eg3:
        c.wait_recv()
    for q in range(GROUPS):
        pl.when(q == opp)(lambda q=q: assemble(q))
    outs[8].start()

    for c in dg2 + dg3:
        c.wait_recv()
    parts = [kinds_of(ag[q, 0].astype(F32), ag[q, 1].astype(F32)) for q in range(GROUPS)]
    for l in range(2):
        for k, out in enumerate((fin, fmix, fexp)):
            out[l] = jnp.concatenate(
                [parts[q][k][12 * l : 12 * l + 12] for q in range(GROUPS)], axis=0
            ).astype(BF16)
        for q in range(GROUPS):
            fred[l, pl.ds(48 * q, 48), :] = jnp.concatenate(
                [parts[q][3][2 * l], parts[q][3][2 * l + 1]], axis=0
            ).astype(BF16)
    for c in outs[4:8]:
        c.start()

    for c in (rs1 + rs2 + rs3 + cf1 + cf2 + cf3 + tp + a1 + a2 + eg1 + eg2 + eg3
              + dg1 + dg2 + dg3):
        c.wait_send()
    for c in outs:
        c.wait()


def flush(*refs):
    sem = refs[18]
    copies = []
    for i in range(9):
        to = refs[9 + i].at[:, 0, :] if i == 7 else refs[9 + i]
        copies.append(pltpu.make_async_copy(refs[i], to, sem.at[i]))
    for c in copies:
        c.start()
    for c in copies:
        c.wait()


def local(
    delta_inputs, delta_mixing, delta_expand, delta_reduce, owner_weights, owner_momentum,
    delta_embed, embed_owner, embed_momentum, basis,
):
    args = (
        delta_inputs[0], delta_mixing[0], delta_expand[0], delta_reduce[0],
        owner_weights.reshape(FLAT_ROWS, 128), owner_momentum.reshape(FLAT_ROWS, 128),
        delta_embed[0],
        jnp.transpose(embed_owner[0], (1, 0, 2)).reshape(3 * ROWS, 1, 128),
        embed_momentum[0, 0].T, basis.T,
    )
    table = jax.ShapeDtypeStruct((3 * ROWS, 128), F32)
    outs = args[:7] + (table, args[8])
    vmem = lambda x: pltpu.VMEM(x.shape, x.dtype)
    dma = pltpu.SemaphoreType.DMA
    half = (48, 1152)
    args = tuple(pltpu.with_memory_space_constraint(x, pltpu.HBM) for x in args)
    results = pl.pallas_call(
        kernel,
        name="outer_step",
        out_shape=[jax.ShapeDtypeStruct(x.shape, x.dtype) for x in outs],
        in_specs=[pl.BlockSpec(memory_space=pltpu.HBM)] * 10,
        out_specs=[pl.BlockSpec(memory_space=pl.ANY)] * 9,
        scratch_shapes=[vmem(x) for x in args[:7] + (table,) + args[8:]]
        + [vmem(x) for x in outs]
        + [
            pltpu.VMEM((GROUPS, 2) + half, BF16),
            pltpu.VMEM((2,) + half, BF16),
            pltpu.VMEM((2,) + half, BF16),
            pltpu.VMEM((4,) + half, BF16),
            pltpu.VMEM((PEERS, 24, 384), BF16),
            pltpu.VMEM((PEERS, 24, 384), BF16),
            pltpu.VMEM((PEERS, 24, 384), BF16),
            pltpu.VMEM((PEERS, 24, 384), BF16),
            pltpu.VMEM((FLAT_ROWS, 128), F32),
            pltpu.VMEM((GROUPS, 2) + half, BF16),
            pltpu.VMEM((GROUPS, SPAN + OVER, 128), F32),
            pltpu.VMEM((GROUPS, 2, HALF, 128), BF16),
            pltpu.VMEM((2, HALF, 128), BF16),
            pltpu.VMEM((2, HALF, 128), BF16),
            pltpu.VMEM((4, HALF, 128), BF16),
            pltpu.VMEM((2, HALF, 128), BF16),
            pltpu.VMEM((2, HALF, 128), BF16),
            pltpu.VMEM((GROUPS, STAGE, WIDTH), BF16),
            dma((10,)),
            dma((9,)),
            dma((24,)),
            dma((24,)),
            dma((PEERS,)),
            dma((PEERS,)),
            dma((PEERS,)),
            dma((PEERS,)),
            dma((2,)),
            dma((2,)),
        ],
        compiler_params=pltpu.CompilerParams(
            collective_id=0, has_side_effects=True, vmem_limit_bytes=26 * 1024 * 1024
        ),
    )(*args)
    results = pl.pallas_call(
        flush,
        name="flush",
        out_shape=[jax.ShapeDtypeStruct(x.shape, x.dtype) for x in args[:9]],
        in_specs=[pl.BlockSpec(memory_space=pl.ANY)] * 9,
        out_specs=[pl.BlockSpec(memory_space=pl.ANY)] * 9,
        scratch_shapes=[dma((9,))],
        compiler_params=pltpu.CompilerParams(vmem_limit_bytes=1024 * 1024),
    )(*results)
    return (
        results[0], results[1], results[2], results[3],
        results[4].reshape(owner_weights.shape), results[5].reshape(owner_momentum.shape),
        results[6],
        jnp.transpose(results[7].reshape(ROWS, 1, WIDTH), (1, 0, 2))[None],
        results[8].T[None, None],
    )


def solution(mesh):
    in_specs = (
        P("rep", None, "shard", "tp"),
        P("rep", None, "shard", "tp"),
        P("rep", None, "shard", "tp"),
        P("rep", None, "shard", "tp"),
        P("rep", "shard", "tp", None),
        P("rep", "shard", "tp", None),
        P("rep", "shard", "tp"),
        P("shard", "rep", None, "tp"),
        P("shard", "rep", None, None),
        P("tp", None),
    )
    out_specs = (
        P(None, "shard", "tp"),
        P(None, "shard", "tp"),
        P(None, "shard", "tp"),
        P(None, "shard", "tp"),
        P("rep", "shard", "tp", None),
        P("rep", "shard", "tp", None),
        P("shard", "tp"),
        P("shard", "rep", None, "tp"),
        P("shard", "rep", None, None),
    )
    return jax.shard_map(local, mesh=mesh, in_specs=in_specs, out_specs=out_specs, check_vma=False)
```
